32 devices in a mesh: seq: 16 (over z, y, core), dp: 2 (over x).
Axes of the slice: x: 2, y: 2, z: 4, core: 2. Of those that a mesh axis runs over, the one named last changes fastest.
Arguments:
- queries: bfloat16 [2, 2048, 1024], P('dp', 'seq'), may hold values from -6 to 6
- keys: bfloat16 [2, 2048, 1024], P('dp', 'seq'), may hold values from -6 to 6
- values: bfloat16 [2, 2048, 1024], P('dp', 'seq'), may hold values from -6 to 6
- d_out: bfloat16 [2, 2048, 1024], P('dp', 'seq'), may hold values from -6 to 6
- segment_ids: int32 [2, 2048], P('dp', 'seq'), may hold values from 0 to 2, never falling along the last dimension, each value on 1 to 1536 neighbouring positions
- block_bucket: int32 [2, 16], P('dp', 'seq'), may hold values from 0 to 63
- block_mask: int32 [2, 16, 5, 1], P('dp', 'seq'), may hold values 0 or 1
- bias_table: bfloat16 [16, 64, 64], replicated, may hold values from -4 to 4
Outputs:
- attention_out: bfloat16 [2, 2048, 1024], P('dp', 'seq')
- d_queries: bfloat16 [2, 2048, 1024], P('dp', 'seq')
- d_keys: bfloat16 [2, 2048, 1024], P('dp', 'seq')
- d_values: bfloat16 [2, 2048, 1024], P('dp', 'seq')
- d_table: float32 [16, 64, 64], replicated
The draws below stay inside these ranges and needn't reach their ends.
Inputs may be any that keep to these rules, and one draw needn't show every extreme that they name: `segment_ids`: each document is a run of consecutive tokens of one sequence.
All inputs are finite; a program needn't handle non-finite values. No bound on the sum of `block_mask` on one device may be relied on, other than what follows from the above.
Results may differ from the reference program's by a relative error of at most 0.024.
Values may be sent and summed in bfloat16 or wider, within the bound.
No kernel may reach another device: no remote copies, remote signals or barrier semaphores. Data moves between devices by JAX's collectives and lax.ppermute only.
A program may use at most 64 MiB of HBM per device.

```python
import math
import jax
import jax.numpy as jnp
import numpy as np
from jax import lax

H = 16
DH = 64
NB = 64
BLK = 128
DOCS = 3
TOK_DEV = 128
HD = 1024
L = 2048
B = 2
NBLK = 16
BPD = 1
LEVELS = 4
N_SEQ = 16


def paired_rows(base_key):
    full_shape = (B, L, HD)
    query_source = jax.random.fold_in(base_key, 101)
    key_source = jax.random.fold_in(base_key, 202)
    query_rows = jnp.clip(jax.random.normal(query_source, full_shape, jnp.float32), -6.0, 6.0)
    key_rows = jnp.clip(jax.random.normal(key_source, full_shape, jnp.float32), -6.0, 6.0)
    return (query_rows, key_rows)


def draw_queries(key, part):
    return paired_rows(key)[0].astype(jnp.bfloat16)


def draw_keys(key, part):
    return paired_rows(key)[1].astype(jnp.bfloat16)


def with_ends(entries, rng, low, high):
    dims = entries.shape
    spot = [jax.random.randint(jax.random.fold_in(rng, axis), (), 0, dims[axis]) for axis in range(len(dims))]
    entries = entries.at[tuple(spot)].set(low)
    longest = dims.index(max(dims))
    spot[longest] = (spot[longest] + 1) % dims[longest]
    return entries.at[tuple(spot)].set(high)


def levels(own_key, dims, cuts, smallest, top_value):
    def one(position, shards_of):
        steps = jax.random.uniform(jax.random.fold_in(jax.random.fold_in(own_key, 6), position), (shards_of,), jnp.float32, smallest / len(cuts), top_value / len(cuts))
        return jnp.repeat(jnp.exp(steps), dims[position] // shards_of).reshape((-1,) + (1,) * (len(dims) - position - 1))

    level = one(*cuts[0])
    for cut in cuts[1:]:
        level = level * one(*cut)
    return level


def split_up(number_of, total, bound, slope):
    weights = [(1 << 20) // math.isqrt(grade ** slope) + 1 for grade in range(2, number_of + 1)]
    surplus, given = total - bound - (number_of - 1), [1] * (number_of - 1)
    while surplus > 0:
        movable = [i for i in range(number_of - 1) if given[i] < bound]
        pool, budget = sum([weights[i] for i in movable]), surplus
        for i in movable:
            extra = min(bound - given[i], max(1, budget * weights[i] // pool), surplus)
            given[i] = given[i] + extra
            surplus = surplus - extra
    return np.array([bound] + given)


def uneven_parts(own_key, amount, total, most, skew):
    if amount == 2:
        one = jax.random.randint(own_key, (), max(1, total - most), min(most, total - 1) + 1)
        return jnp.stack([one, total - one])
    lengths = jnp.asarray(split_up(amount, total, most, skew), jnp.int32)
    pairs = (amount - 1) // 2
    source_of, sink = lengths[1:1 + 2 * pairs:2], lengths[2:2 + 2 * pairs:2]
    margin = jnp.minimum(source_of - 1, most - sink)
    moved = jax.random.randint(jax.random.fold_in(own_key, 1), (pairs,), 0, 1 << 20) % (margin + 1)
    lengths = lengths.at[1:1 + 2 * pairs:2].set(source_of - moved).at[2:2 + 2 * pairs:2].set(sink + moved)
    return lengths[jax.random.permutation(jax.random.fold_in(own_key, 2), amount)]


def noise(own_key, dims, scale, bound, pieces=(), kind=jnp.bfloat16):
    entries = scale * jax.random.normal(own_key, dims, jnp.float32)
    if pieces:
        entries = entries * levels(own_key, dims, pieces, -0.22, 0.18)
    return jnp.clip(entries, -bound, bound).astype(kind)


def setup_inputs(seed: int = 0) -> dict:
    key_list = jax.random.split(jax.random.key(seed), 9)
    return {
        "queries": draw_queries(jax.random.fold_in(key_list[8], 71), 0),
        "keys": draw_keys(jax.random.fold_in(key_list[8], 71), 0),
        "values": noise(key_list[2], (B, L, HD), 1.0, 6.0, ((0, 2), (1, 16))),
        "d_out": noise(key_list[3], (B, L, HD), 1.0, 6.0, ((0, 2), (1, 16))),
        "segment_ids": jax.vmap(lambda own: jnp.searchsorted(jnp.cumsum(uneven_parts(own, DOCS, L, 3 * L // 4, 0)), jnp.arange(L), side="right"))(jax.random.split(key_list[4], B)).reshape((B, L)).astype(jnp.int32),
        "block_bucket": with_ends(jax.random.randint(key_list[5], (B, NBLK), 0, NB), jax.random.fold_in(key_list[5], 1), 0, NB - 1).astype(jnp.int32),
        "block_mask": with_ends((jax.random.randint(key_list[6], (B, NBLK, LEVELS + 1, BPD), 0, 4) < 3).astype(jnp.int32), jax.random.fold_in(key_list[6], 1), 0, 1),
        "bias_table": noise(key_list[7], (H, NB, NB), 1.0, 4.0),
    }


masked_value = -1.0e30


def expand_blocks(bias_block, row_count, col_count):
    leading = bias_block.shape[:-2]
    row_blocks = bias_block.shape[-2]
    col_blocks = bias_block.shape[-1]
    widened = jnp.broadcast_to(bias_block[..., :, None, :, None], leading + (row_blocks, row_count // row_blocks, col_blocks, col_count // col_blocks))
    return widened.reshape(leading + (row_count, col_count))


def round_low(array):
    return lax.optimization_barrier(array.astype(jnp.bfloat16)).astype(jnp.float32)


def take_device(array, device_id):
    return lax.dynamic_index_in_dim(array, device_id, 0, keepdims=False)


def reference(queries, keys, values, d_out, segment_ids, block_bucket, block_mask, bias_table):
    bias_wide = bias_table.astype(jnp.float32)
    xor_masks = [0] + [1 << level for level in range(LEVELS)]
    outputs = []
    grads_query = []
    grads_key = []
    grads_value = []
    table_grad = jnp.zeros((H, NB, NB), jnp.float32)
    for batch_id in range(B):
        query_dev = queries[batch_id].astype(jnp.float32).reshape(N_SEQ, TOK_DEV, H, DH)
        key_dev = keys[batch_id].astype(jnp.float32).reshape(N_SEQ, TOK_DEV, H, DH)
        value_dev = values[batch_id].astype(jnp.float32).reshape(N_SEQ, TOK_DEV, H, DH)
        grad_dev = d_out[batch_id].astype(jnp.float32).reshape(N_SEQ, TOK_DEV, H, DH)
        seg_dev = segment_ids[batch_id].reshape(N_SEQ, TOK_DEV)
        bucket_dev = block_bucket[batch_id].reshape(N_SEQ, BPD)
        mask_dev = block_mask[batch_id].reshape(N_SEQ, BPD, LEVELS + 1, BPD)

        def device_step(state_in, device_id):
            key_acc, value_acc, table_acc = state_in
            partners = [jnp.bitwise_xor(device_id, value) for value in xor_masks]
            query_heads = take_device(query_dev, device_id)
            grad_heads = take_device(grad_dev, device_id)
            seg_rows = take_device(seg_dev, device_id)
            bucket_rows = take_device(bucket_dev, device_id)
            mask_rows = take_device(mask_dev, device_id)
            score_parts = []
            allow_parts = []
            key_parts = []
            value_parts = []
            bucket_parts = []
            for section_num, partner in enumerate(partners):
                key_heads = take_device(key_dev, partner)
                value_heads = take_device(value_dev, partner)
                seg_cols = take_device(seg_dev, partner)
                bucket_cols = take_device(bucket_dev, partner)
                block_ok = mask_rows[:, section_num, :] != 0
                if section_num == 0:
                    block_ok = block_ok | jnp.eye(BPD, dtype=bool)
                allowed = (seg_rows[:, None] == seg_cols[None, :]) & expand_blocks(block_ok, TOK_DEV, TOK_DEV)
                bias_block = bias_wide[:, bucket_rows[:, None], bucket_cols[None, :]]
                products = jnp.einsum("thd,uhd->htu", query_heads, key_heads)
                shifted = products * 0.125 + expand_blocks(bias_block, TOK_DEV, TOK_DEV)
                score_parts.append(jnp.where(allowed[None], shifted, masked_value))
                allow_parts.append(allowed)
                key_parts.append(key_heads)
                value_parts.append(value_heads)
                bucket_parts.append(bucket_cols)
            scores = jnp.concatenate(score_parts, axis=2)
            allowed = jnp.concatenate(allow_parts, axis=1)
            key_all = jnp.concatenate(key_parts, axis=0)
            value_all = jnp.concatenate(value_parts, axis=0)
            bucket_all = jnp.concatenate(bucket_parts, axis=0)
            row_max = jnp.max(scores, axis=-1)
            weights = jnp.where(allowed[None], jnp.exp(scores - row_max[:, :, None]), 0.0)
            row_sum = jnp.sum(weights, axis=-1)
            weights_low = round_low(weights)
            attended = jnp.einsum("htu,uhd->thd", weights_low, value_all) / row_sum.T[:, :, None]
            out_low = attended.astype(jnp.bfloat16)
            lse = row_max + jnp.log(row_sum)
            probs = jnp.where(allowed[None], jnp.exp(scores - lse[:, :, None]), 0.0)
            probs_low = round_low(probs)
            dprob = jnp.einsum("thd,uhd->htu", grad_heads, value_all)
            row_delta = jnp.sum(out_low.astype(jnp.float32) * grad_heads, axis=-1).T
            dscore = probs * (dprob - row_delta[:, :, None])
            dscore_low = round_low(dscore)
            grad_query = (jnp.einsum("htu,uhd->thd", dscore_low, key_all) * 0.125).astype(jnp.bfloat16)
            key_term = jnp.einsum("htu,thd->uhd", dscore_low, query_heads) * 0.125
            value_term = jnp.einsum("htu,thd->uhd", probs_low, grad_heads)
            for section_num, partner in enumerate(partners):
                key_portion = key_term[section_num * TOK_DEV:(section_num + 1) * TOK_DEV]
                value_portion = value_term[section_num * TOK_DEV:(section_num + 1) * TOK_DEV]
                if section_num > 0:
                    key_portion = round_low(key_portion)
                    value_portion = round_low(value_portion)
                key_acc = key_acc.at[partner].add(key_portion)
                value_acc = value_acc.at[partner].add(value_portion)
            block_sums = dscore.reshape(H, BPD, BLK, (LEVELS + 1) * BPD, BLK).sum(axis=(2, 4))
            table_acc = table_acc.at[:, bucket_rows[:, None], bucket_all[None, :]].add(block_sums)
            return (key_acc, value_acc, table_acc), (out_low, grad_query)

        start = (jnp.zeros((N_SEQ, TOK_DEV, H, DH), jnp.float32), jnp.zeros((N_SEQ, TOK_DEV, H, DH), jnp.float32), table_grad)
        state_out, stacked = lax.scan(device_step, start, jnp.arange(N_SEQ, dtype=jnp.int32))
        key_acc, value_acc, table_grad = state_out
        outputs.append(stacked[0].reshape(L, HD))
        grads_query.append(stacked[1].reshape(L, HD))
        grads_key.append(key_acc.astype(jnp.bfloat16).reshape(L, HD))
        grads_value.append(value_acc.astype(jnp.bfloat16).reshape(L, HD))
    return (jnp.stack(outputs), jnp.stack(grads_query), jnp.stack(grads_key), jnp.stack(grads_value), table_grad)
```

```python
import functools

import jax
import jax.numpy as jnp
from jax import lax
from jax.experimental import pallas as pl
from jax.experimental.pallas import tpu as pltpu
from jax.sharding import PartitionSpec as P

H = 16
DH = 64
NB = 64
BLK = 128
HALVES = 2
INFO = 8
LANES = 128
PAIR_LANES = 2 * DH
BUCKET_LANE = 112
MASKED = -1e30

F32 = jnp.float32
BF16 = jnp.bfloat16


def contract(a, b, dim_a, dim_b):
    return lax.dot_general(a, b, (((dim_a,), (dim_b,)), ((), ())), preferred_element_type=F32)


def from_partner(value, axis, mask):
    pairs = [(source, source ^ mask) for source in range(lax.axis_size(axis))]
    return lax.ppermute(value, axis, pairs)


def lane_iota(shape):
    return lax.broadcasted_iota(jnp.int32, shape, len(shape) - 1)


def row_iota(shape):
    return lax.broadcasted_iota(jnp.int32, shape, len(shape) - 2)


def split_pair(pair, low):
    zero = jnp.zeros_like(pair)
    return jnp.concatenate([jnp.where(low, pair, zero), jnp.where(low, zero, pair)], axis=0)


def attention_body(section_count, half, first, *refs):
    level_count = section_count - 1
    refs = list(refs)

    def take(count):
        taken, refs[:] = refs[:count], refs[count:]
        return taken

    mask_ref, bucket_ref, seg_ref, table_ref = take(4)
    q_ref, do_ref, k_ref, v_ref = take(4)
    partner_refs = take(level_count)
    info_refs = partner_refs if first else take(level_count)
    if not first:
        pay_in_ref, _, _ = take(3)
    out_ref, dq_ref, own_ref, pay_ref = take(4)
    term_refs = take(level_count)
    masks, biases = take(2)
    pair = pl.program_id(0)
    half_heads = biases.shape[1]

    @pl.when(pair == 0)
    def _():
        seg_rows = seg_ref[...].astype(F32)
        own_bucket = bucket_ref[0]
        in_row = row_iota((half_heads, NB, LANES)) == own_bucket
        pay = jnp.zeros((1, LANES), F32) if first else pay_in_ref[...]
        for s in range(section_count):
            if s == 0:
                seg_cols = seg_rows
                bucket = jnp.full((1, LANES), own_bucket, jnp.int32).astype(F32)
            else:
                info = info_refs[s - 1][2 * BLK : 2 * BLK + INFO, :].astype(F32)
                seg_cols = info[0:1]
                bucket = info[1:2]
            cols = jnp.broadcast_to(seg_cols, (BLK, BLK)).T
            same = cols == seg_rows
            open_block = MASKED if s == 0 else jnp.where(mask_ref[s] != 0, 0.0, MASKED)
            masks[s * BLK : (s + 1) * BLK, :] = jnp.where(
                same, jnp.full((BLK, BLK), 0.0 if s == 0 else open_block, F32), MASKED
            )
            hot = (row_iota((NB, LANES)).astype(F32) == bucket).astype(BF16)
            picked = contract(table_ref[...], hot, 1, 0).reshape(half_heads, NB, LANES)
            biases[s] = jnp.sum(jnp.where(in_row, picked, 0.0), axis=1)
            if first:
                pay = jnp.where(lane_iota(pay.shape) == BUCKET_LANE + s, bucket, pay)
        pay_ref[...] = pay

    low = lane_iota((BLK, PAIR_LANES)) < DH
    q_stack = split_pair(q_ref[...] * jnp.asarray(0.125, BF16), low)
    key_list = [k_ref[...]] + [r[0:BLK, :] for r in partner_refs]
    value_list = [v_ref[...]] + [r[BLK : 2 * BLK, :] for r in partner_refs]
    shifts = []
    scores = []
    top = None
    for s in range(section_count):
        mask = masks[s * BLK : (s + 1) * BLK, :]
        score = contract(key_list[s], q_stack, 1, 1) + jnp.concatenate([mask, mask], axis=1)
        bias = jnp.concatenate(
            [biases[s, pl.ds(2 * pair, 1), :], biases[s, pl.ds(2 * pair + 1, 1), :]], axis=1
        )
        best = jnp.max(score, axis=0, keepdims=True) + bias
        top = best if top is None else jnp.maximum(top, best)
        scores.append(score)
        shifts.append(bias)
    weights = []
    weights_low = []
    total = None
    out_stack = None
    for s in range(section_count):
        weight = jnp.exp(scores[s] - (top - shifts[s]))
        weight_low = weight.astype(BF16)
        part = jnp.sum(weight, axis=0, keepdims=True)
        total = part if total is None else total + part
        term = contract(weight_low, value_list[s], 0, 0)
        out_stack = term if out_stack is None else out_stack + term
        weights.append(weight)
        weights_low.append(weight_low)
    inverse = 1.0 / total
    inverse_cols = jnp.broadcast_to(inverse, (BLK, 2 * BLK)).T
    scaled = out_stack * inverse_cols
    out_low = jnp.where(low, scaled[:BLK], scaled[BLK:]).astype(BF16)
    out_ref[...] = out_low
    grad = do_ref[...].astype(F32)
    products = (out_low.astype(F32) * grad).T
    delta = jnp.concatenate(
        [
            jnp.sum(products[:DH], axis=0, keepdims=True),
            jnp.sum(products[DH:], axis=0, keepdims=True),
        ],
        axis=1,
    )
    delta = delta * inverse
    grad_stack = jnp.concatenate(
        [
            jnp.where(low, grad * inverse_cols[:BLK], 0.0),
            jnp.where(low, 0.0, grad * inverse_cols[BLK:]),
        ],
        axis=0,
    ).astype(BF16)
    dq_stack = None
    pay = pay_ref[...]
    lanes = lane_iota((1, LANES))
    head = half * half_heads + 2 * pair
    for s in range(section_count):
        dprob = contract(value_list[s], grad_stack, 1, 1)
        dscore = weights[s] * (dprob - delta)
        dscore_low = dscore.astype(BF16)
        sums = jnp.sum(dscore, axis=0, keepdims=True)
        even = jnp.sum(sums[:, :BLK], axis=1, keepdims=True)
        odd = jnp.sum(sums[:, BLK:], axis=1, keepdims=True)
        pay = jnp.where(lanes == s * H + head, even, pay)
        pay = jnp.where(lanes == s * H + head + 1, odd, pay)
        term = contract(dscore_low, key_list[s], 0, 0)
        dq_stack = term if dq_stack is None else dq_stack + term
        key_term = contract(dscore_low, q_stack, 1, 0)
        value_term = contract(weights_low[s], grad_stack, 1, 0)
        if s == 0:
            own_ref[0:BLK, :] = key_term
            own_ref[BLK : 2 * BLK, :] = value_term
        else:
            term_refs[s - 1][0:BLK, :] = key_term.astype(BF16)
            term_refs[s - 1][BLK : 2 * BLK, :] = value_term.astype(BF16)
    pay_ref[...] = pay
    dq_ref[...] = (jnp.where(low, dq_stack[:BLK], dq_stack[BLK:]) * 0.125).astype(BF16)


def attention_half(half, scalars, table_rows, rows, partners, infos, previous):
    section_count = len(partners) + 1
    level_count = section_count - 1
    row_count, feature_count = rows[0].shape
    half_features = feature_count // HALVES
    pairs = half_features // PAIR_LANES
    half_heads = half_features // DH
    first = previous is None
    mask, bucket, seg = scalars

    def whole(shape):
        return pl.BlockSpec(shape, lambda j: (0,) * len(shape))

    row_spec = pl.BlockSpec((row_count, PAIR_LANES), lambda j: (0, half * pairs + j))

    def column_spec(array):
        return pl.BlockSpec((array.shape[0], PAIR_LANES), lambda j: (0, j))

    smem = pl.BlockSpec(memory_space=pltpu.SMEM)
    operands = [mask, bucket, seg, table_rows, *rows, *partners]
    in_specs = [
        smem,
        smem,
        whole(seg.shape),
        pl.BlockSpec((half_heads * NB, NB), lambda j: (half, 0)),
        *[row_spec] * 4,
        *[column_spec(p) for p in partners],
    ]
    aliases = {}
    if not first:
        operands += [*infos, previous[3], previous[0], previous[1]]
        in_specs += [pl.BlockSpec((p.shape[0], PAIR_LANES), lambda j: (0, 0)) for p in infos]
        in_specs += [whole((1, LANES))] + [pl.BlockSpec(memory_space=pl.ANY)] * 2
        aliases = {len(operands) - 2: 0, len(operands) - 1: 1}
    packed = jax.ShapeDtypeStruct((2 * row_count, half_features), BF16)
    out_shape = [
        jax.ShapeDtypeStruct((row_count, feature_count), BF16),
        jax.ShapeDtypeStruct((row_count, feature_count), BF16),
        jax.ShapeDtypeStruct((2 * row_count, half_features), F32),
        jax.ShapeDtypeStruct((1, LANES), F32),
        *[packed] * level_count,
    ]
    out_specs = [
        row_spec,
        row_spec,
        column_spec(out_shape[2]),
        whole((1, LANES)),
        *[column_spec(packed)] * level_count,
    ]
    return pl.pallas_call(
        functools.partial(attention_body, section_count, half, first),
        grid=(pairs,),
        in_specs=in_specs,
        out_specs=out_specs,
        out_shape=out_shape,
        scratch_shapes=[
            pltpu.VMEM((section_count * BLK, BLK), F32),
            pltpu.VMEM((section_count, half_heads, LANES), F32),
        ],
        input_output_aliases=aliases,
        compiler_params=pltpu.CompilerParams(dimension_semantics=("arbitrary",)),
        cost_estimate=pl.CostEstimate(
            flops=12 * section_count * half_heads * BLK * BLK * DH,
            bytes_accessed=4 * 2**20,
            transcendentals=section_count * half_heads * BLK * BLK,
        ),
        name="attention",
    )(*operands)


def finish_body(level_count, *refs):
    own_ref = refs[0]
    term_refs = refs[1 : 1 + level_count]
    key_ref, value_ref = refs[-2:]
    total = own_ref[...]
    for term in term_refs:
        total = total + term[...].astype(F32)
    total = total.astype(BF16)
    key_ref[...] = total[:BLK]
    value_ref[...] = total[BLK:]


def finish_half(half, own, terms, previous):
    row_count = own.shape[0] // 2
    half_features = own.shape[1]
    feature_count = half_features * HALVES
    step = 2 * PAIR_LANES
    steps = half_features // step
    column = pl.BlockSpec((2 * row_count, step), lambda j: (0, j))
    out_spec = pl.BlockSpec((row_count, step), lambda j: (0, half * steps + j))
    out = jax.ShapeDtypeStruct((row_count, feature_count), BF16)
    operands = [own, *terms]
    in_specs = [column] * len(operands)
    aliases = {}
    if previous is not None:
        operands += list(previous)
        in_specs += [pl.BlockSpec(memory_space=pl.ANY)] * 2
        aliases = {len(operands) - 2: 0, len(operands) - 1: 1}
    return pl.pallas_call(
        functools.partial(finish_body, len(terms)),
        grid=(steps,),
        in_specs=in_specs,
        out_specs=[out_spec, out_spec],
        out_shape=[out, out],
        input_output_aliases=aliases,
        compiler_params=pltpu.CompilerParams(dimension_semantics=("arbitrary",)),
        cost_estimate=pl.CostEstimate(flops=2**19, bytes_accessed=2**21, transcendentals=0),
        name="finish",
    )(*operands)


def table_body(section_count, gathered_ref, table_ref):
    gathered = gathered_ref[...]
    count = gathered.shape[0]
    lanes = lane_iota((count, PAIR_LANES))
    column = jnp.where(lanes < NB, lanes, lanes - NB).astype(F32)
    row_hot = (lane_iota((count, NB)).astype(F32) == gathered[:, BUCKET_LANE : BUCKET_LANE + 1]).astype(F32)
    rows = jnp.concatenate([row_hot] * section_count, axis=0)
    hots = [
        column == gathered[:, BUCKET_LANE + s : BUCKET_LANE + s + 1] for s in range(section_count)
    ]
    for pair in range(H // 2):
        parts = []
        for s in range(section_count):
            lane = s * H + 2 * pair
            value = jnp.where(lanes < NB, gathered[:, lane : lane + 1], gathered[:, lane + 1 : lane + 2])
            parts.append(jnp.where(hots[s], value, 0.0))
        tile = lax.dot_general(
            rows,
            jnp.concatenate(parts, axis=0),
            (((0,), (0,)), ((), ())),
            preferred_element_type=F32,
            precision=lax.Precision.HIGHEST,
        )
        table_ref[2 * pair] = tile[:, :NB]
        table_ref[2 * pair + 1] = tile[:, NB:]


def table_of(payload, section_count):
    gathered = payload
    for axis in ("dp", "seq"):
        mask = 1
        while mask < lax.axis_size(axis):
            gathered = jnp.concatenate([gathered, from_partner(gathered, axis, mask)], axis=0)
            mask *= 2
    return pl.pallas_call(
        functools.partial(table_body, section_count),
        out_shape=jax.ShapeDtypeStruct((H, NB, NB), F32),
        name="table",
    )(gathered)


def local(queries, keys, values, d_out, segment_ids, block_bucket, block_mask, bias_table):
    feature_count = queries.shape[2]
    half_features = feature_count // HALVES
    level_count = lax.axis_size("seq").bit_length() - 1
    section_count = level_count + 1
    rows = [queries[0], d_out[0], keys[0], values[0]]
    own_keys, own_values = rows[2], rows[3]
    scalars = (block_mask.reshape(-1), block_bucket.reshape(-1), segment_ids)
    table_rows = bias_table.reshape(H * NB, NB)
    seg_line = jnp.tile(segment_ids.astype(BF16), (1, half_features // BLK))
    bucket_line = jnp.broadcast_to(block_bucket.astype(BF16), (INFO - 1, half_features))
    info = jnp.concatenate([seg_line, bucket_line], axis=0)
    packs = []
    for half in range(HALVES):
        window = slice(half * half_features, (half + 1) * half_features)
        pieces = [own_keys[:, window], own_values[:, window]]
        packs.append(jnp.concatenate(pieces + ([info] if half == 0 else []), axis=0))
    arrived = [[None] * level_count for _ in range(HALVES)]
    for half in range(HALVES):
        for level in reversed(range(level_count)):
            arrived[half][level] = from_partner(packs[half], "seq", 1 << level)
    result = None
    finished = None
    for half in range(HALVES):
        result = attention_half(
            half, scalars, table_rows, rows, arrived[half], arrived[0], result
        )
        back = [None] * level_count
        for level in reversed(range(level_count)):
            back[level] = from_partner(result[4 + level], "seq", 1 << level)
        finished = finish_half(half, result[2], back, finished)
    table_total = table_of(result[3], section_count)
    return (result[0][None], result[1][None], finished[0][None], finished[1][None], table_total)


def solution(mesh):
    rows = P("dp", "seq", None)
    in_specs = (
        rows,
        rows,
        rows,
        rows,
        P("dp", "seq"),
        P("dp", "seq"),
        P("dp", "seq", None, None),
        P(),
    )
    return jax.shard_map(
        local, mesh=mesh, in_specs=in_specs, out_specs=(rows,) * 4 + (P(),), check_vma=False
    )
```

```python
import functools

import jax
import jax.numpy as jnp
from jax import lax
from jax.experimental import pallas as pl
from jax.experimental.pallas import tpu as pltpu
from jax.sharding import PartitionSpec as P

H = 16
DH = 64
NB = 64
BLK = 128
HALVES = 2
INFO = 8
LANES = 128
PAIR_LANES = 2 * DH
BUCKET_LANE = 112
MASKED = -1e30
UNROLL = 4
VMEM_LIMIT = 24 * 2**20
FLOPS = 2 * 10**10

F32 = jnp.float32
BF16 = jnp.bfloat16


def contract(a, b, dim_a, dim_b):
    return lax.dot_general(a, b, (((dim_a,), (dim_b,)), ((), ())), preferred_element_type=F32)


def from_partner(value, axis, mask):
    pairs = [(source, source ^ mask) for source in range(lax.axis_size(axis))]
    return lax.ppermute(value, axis, pairs)


def lane_iota(shape):
    return lax.broadcasted_iota(jnp.int32, shape, len(shape) - 1)


def row_iota(shape):
    return lax.broadcasted_iota(jnp.int32, shape, len(shape) - 2)


def split_pair(pair, low):
    zero = jnp.zeros_like(pair)
    return jnp.concatenate([jnp.where(low, pair, zero), jnp.where(low, zero, pair)], axis=0)


def attention_body(near_count, far_count, half, *refs):
    section_count = 1 + near_count + far_count
    first = half == 0
    refs = list(refs)

    def take(count):
        taken, refs[:] = refs[:count], refs[count:]
        return taken

    mask_ref, bucket_ref, seg_ref, table_ref, q_ref, do_ref, k_ref, v_ref = take(8)
    near_refs = take(near_count)
    far_refs = take(far_count)
    if not first:
        masks, biases, pay_in_ref = take(3)
        earlier = take(2 + near_count)
    out_ref, dq_ref = take(2)
    near_out_refs = take(near_count)
    own_ref, *far_out_refs, pay_ref = take(2 + far_count)
    if first:
        masks, biases = take(2)
    half_features = far_refs[0].shape[1]
    half_heads = half_features // DH

    if first:
        own_bucket = bucket_ref[0]
        seg_rows = seg_ref[...].astype(F32)
        in_row = row_iota((H, NB, LANES)) == own_bucket
        pay = jnp.zeros((1, LANES), F32)
        for s in range(section_count):
            if s == 0:
                seg_cols = seg_rows
                bucket = jnp.full((1, LANES), own_bucket, jnp.int32).astype(F32)
                shut = 0.0
            else:
                source = near_refs[s - 1] if s <= near_count else far_refs[s - 1 - near_count]
                info = source[2 * BLK : 2 * BLK + INFO, 0:LANES].astype(F32)
                seg_cols = info[0:1]
                bucket = info[1:2]
                shut = jnp.where(mask_ref[s] != 0, 0.0, MASKED)
            cols = jnp.broadcast_to(seg_cols, (BLK, BLK)).T
            masks[s * BLK : (s + 1) * BLK, :] = jnp.where(
                cols == seg_rows, jnp.full((BLK, BLK), shut, F32), MASKED
            )
            hot = (row_iota((NB, LANES)).astype(F32) == bucket).astype(BF16)
            picked = contract(table_ref[...], hot, 1, 0).reshape(H, NB, LANES)
            biases[s] = jnp.sum(jnp.where(in_row, picked, 0.0), axis=1)
            pay = jnp.where(lane_iota(pay.shape) == BUCKET_LANE + s, bucket, pay)
        pay_ref[...] = pay
    else:
        pay_ref[...] = pay_in_ref[...]
        for source, target in zip(earlier, [out_ref, dq_ref, *near_out_refs]):
            target[:, 0 : half * half_features] = source[...]

    low = lane_iota((BLK, PAIR_LANES)) < DH
    lanes = lane_iota((1, LANES))

    def one_pair(pair, carry):
        here = pl.ds(pl.multiple_of(pair * PAIR_LANES, PAIR_LANES), PAIR_LANES)
        there = pl.ds(
            pl.multiple_of(half * half_features + pair * PAIR_LANES, PAIR_LANES), PAIR_LANES
        )
        mine = here if first else there
        head = half * half_heads + 2 * pair
        q_stack = split_pair(q_ref[:, there] * jnp.asarray(0.125, BF16), low)
        grad_stack = split_pair(do_ref[:, there], low)
        key_rows = jnp.concatenate(
            [k_ref[:, there]]
            + [r[0:BLK, there] for r in near_refs]
            + [r[0:BLK, here] for r in far_refs],
            axis=0,
        )
        value_rows = jnp.concatenate(
            [v_ref[:, there]]
            + [r[BLK : 2 * BLK, there] for r in near_refs]
            + [r[BLK : 2 * BLK, here] for r in far_refs],
            axis=0,
        )
        raw = contract(key_rows, q_stack, 1, 1)
        dprob = contract(value_rows, grad_stack, 1, 1)
        scores = []
        shifts = []
        top = None
        for s in range(section_count):
            block = slice(s * BLK, (s + 1) * BLK)
            mask = masks[block, :]
            score = raw[block] + jnp.concatenate([mask, mask], axis=1)
            bias = jnp.concatenate(
                [biases[s, pl.ds(head, 1), :], biases[s, pl.ds(head + 1, 1), :]], axis=1
            )
            best = jnp.max(score, axis=0, keepdims=True) + bias
            top = best if top is None else jnp.maximum(top, best)
            scores.append(score)
            shifts.append(bias)
        weights = [jnp.exp(scores[s] - (top - shifts[s])) for s in range(section_count)]
        total = sum(jnp.sum(weight, axis=0, keepdims=True) for weight in weights)
        inverse = 1.0 / total
        probs = [weight * inverse for weight in weights]
        probs_low = jnp.concatenate([prob.astype(BF16) for prob in probs], axis=0)
        out_stack = contract(probs_low, value_rows, 0, 0)
        pulls = [probs[s] * dprob[s * BLK : (s + 1) * BLK] for s in range(section_count)]
        delta = sum(jnp.sum(pull, axis=0, keepdims=True) for pull in pulls)
        dscores = [pulls[s] - probs[s] * delta for s in range(section_count)]
        dscore_low = jnp.concatenate([dscore.astype(BF16) for dscore in dscores], axis=0)
        value_terms = contract(probs_low, grad_stack, 1, 0)
        key_terms = contract(dscore_low, q_stack, 1, 0)
        dq_stack = contract(dscore_low, key_rows, 0, 0)
        out_ref[:, mine] = jnp.where(low, out_stack[:BLK], out_stack[BLK:]).astype(BF16)
        dq_ref[:, mine] = (jnp.where(low, dq_stack[:BLK], dq_stack[BLK:]) * 0.125).astype(BF16)
        pay = pay_ref[...]
        for s in range(section_count):
            sums = jnp.sum(dscores[s], axis=0, keepdims=True)
            even = jnp.sum(sums[:, :BLK], axis=1, keepdims=True)
            odd = jnp.sum(sums[:, BLK:], axis=1, keepdims=True)
            pay = jnp.where(lanes == s * H + head, even, pay)
            pay = jnp.where(lanes == s * H + head + 1, odd, pay)
            key_term = key_terms[s * BLK : (s + 1) * BLK]
            value_term = value_terms[s * BLK : (s + 1) * BLK]
            if s == 0:
                own_ref[0:BLK, here] = key_term
                own_ref[BLK : 2 * BLK, here] = value_term
            elif s <= near_count:
                near_out_refs[s - 1][0:BLK, mine] = key_term.astype(BF16)
                near_out_refs[s - 1][BLK : 2 * BLK, mine] = value_term.astype(BF16)
            else:
                far_out_refs[s - 1 - near_count][0:BLK, here] = key_term.astype(BF16)
                far_out_refs[s - 1 - near_count][BLK : 2 * BLK, here] = value_term.astype(BF16)
        pay_ref[...] = pay
        return carry

    lax.fori_loop(0, half_features // PAIR_LANES, one_pair, 0, unroll=UNROLL)


def attention_half(half, scalars, table_rows, rows, near, far, previous):
    near_count, far_count = len(near), len(far)
    section_count = 1 + near_count + far_count
    row_count, feature_count = rows[0].shape
    half_features = feature_count // HALVES
    half_heads = half_features // DH
    smem = pl.BlockSpec(memory_space=pltpu.SMEM)
    vmem = pl.BlockSpec(memory_space=pltpu.VMEM)
    operands = [*scalars, table_rows, *rows, *near, *far]
    in_specs = [smem, smem] + [vmem] * (len(operands) - 2)
    covered = (half + 1) * half_features
    packed = jax.ShapeDtypeStruct((2 * row_count, half_features), BF16)
    out_shape = [
        *[jax.ShapeDtypeStruct((row_count, covered), BF16)] * 2,
        *[jax.ShapeDtypeStruct((2 * row_count, covered), BF16)] * near_count,
        jax.ShapeDtypeStruct((2 * row_count, half_features), F32),
        *[packed] * far_count,
        jax.ShapeDtypeStruct((1, LANES), F32),
    ]
    if previous is None:
        out_shape += [
            jax.ShapeDtypeStruct((section_count * BLK, BLK), F32),
            jax.ShapeDtypeStruct((section_count, H, LANES), F32),
        ]
    else:
        operands += [*previous[-2:], previous[-3], *previous[: 2 + near_count]]
        in_specs += [vmem] * (5 + near_count)
    return pl.pallas_call(
        functools.partial(attention_body, near_count, far_count, half),
        in_specs=in_specs,
        out_specs=[vmem] * len(out_shape),
        out_shape=out_shape,
        compiler_params=pltpu.CompilerParams(vmem_limit_bytes=VMEM_LIMIT),
        cost_estimate=pl.CostEstimate(
            flops=FLOPS, bytes_accessed=4 * 2**20, transcendentals=section_count * half_heads * BLK * BLK
        ),
        name="attention",
    )(*operands)


def finish_body(near_count, far_count, *refs):
    own_refs = refs[:HALVES]
    near_refs = refs[HALVES : HALVES + near_count]
    far_refs = refs[HALVES + near_count : -2]
    key_ref, value_ref = refs[-2:]
    half_features = far_refs[0].shape[1]
    for half in range(HALVES):
        window = slice(half * half_features, (half + 1) * half_features)
        for out_ref, block in ((key_ref, slice(0, BLK)), (value_ref, slice(BLK, 2 * BLK))):
            total = own_refs[half][block, :]
            for ref in near_refs:
                total = total + ref[block, window].astype(F32)
            for ref in far_refs[half * far_count : (half + 1) * far_count]:
                total = total + ref[block, :].astype(F32)
            out_ref[:, window] = total.astype(BF16)


def finish(own, near, far):
    row_count = own[0].shape[0] // 2
    vmem = pl.BlockSpec(memory_space=pltpu.VMEM)
    out = jax.ShapeDtypeStruct((row_count, HALVES * own[0].shape[1]), BF16)
    return pl.pallas_call(
        functools.partial(finish_body, len(near), len(far) // HALVES),
        in_specs=[vmem] * (HALVES + len(near) + len(far)),
        out_specs=[vmem, vmem],
        out_shape=[out, out],
        compiler_params=pltpu.CompilerParams(vmem_limit_bytes=VMEM_LIMIT),
        cost_estimate=pl.CostEstimate(flops=2**19, bytes_accessed=2**21, transcendentals=0),
        name="finish",
    )(*own, *near, *far)


def table_body(section_count, *refs):
    table_ref = refs[-1]
    gathered = jnp.concatenate([ref[...] for ref in refs[:-1]], axis=0)
    count = gathered.shape[0]
    lanes = lane_iota((count, PAIR_LANES))
    column = jnp.where(lanes < NB, lanes, lanes - NB).astype(F32)
    bucket = gathered[:, BUCKET_LANE : BUCKET_LANE + 1]
    row_hot = (lane_iota((count, NB)).astype(F32) == bucket).astype(F32)
    rows = jnp.concatenate([row_hot] * section_count, axis=0)
    hots = [
        column == gathered[:, BUCKET_LANE + s : BUCKET_LANE + s + 1] for s in range(section_count)
    ]
    for pair in range(H // 2):
        parts = []
        for s in range(section_count):
            lane = s * H + 2 * pair
            value = jnp.where(lanes < NB, gathered[:, lane : lane + 1], gathered[:, lane + 1 : lane + 2])
            parts.append(jnp.where(hots[s], value, 0.0))
        tile = lax.dot_general(
            rows,
            jnp.concatenate(parts, axis=0),
            (((0,), (0,)), ((), ())),
            preferred_element_type=F32,
            precision=lax.Precision.HIGHEST,
        )
        table_ref[2 * pair] = tile[:, :NB]
        table_ref[2 * pair + 1] = tile[:, NB:]


def table_of(blocks, section_count):
    vmem = pl.BlockSpec(memory_space=pltpu.VMEM)
    return pl.pallas_call(
        functools.partial(table_body, section_count),
        in_specs=[vmem] * len(blocks),
        out_specs=vmem,
        out_shape=jax.ShapeDtypeStruct((H, NB, NB), F32),
        compiler_params=pltpu.CompilerParams(vmem_limit_bytes=VMEM_LIMIT),
        name="table",
    )(*blocks)


def pack_body(bucket_ref, seg_ref, key_ref, value_ref, whole_ref, first_ref, second_ref):
    half_features = first_ref.shape[1]
    top = row_iota((INFO, LANES)) == 0
    bucket = jnp.full((INFO, LANES), bucket_ref[0], jnp.int32)
    info = jnp.where(top, seg_ref[...], bucket).astype(F32).astype(BF16)
    for block, source in ((slice(0, BLK), key_ref), (slice(BLK, 2 * BLK), value_ref)):
        whole_ref[block, :] = source[...]
        first_ref[block, :] = source[:, :half_features]
        second_ref[block, :] = source[:, half_features:]
    for target in (whole_ref, first_ref):
        for start in range(0, target.shape[1], LANES):
            target[2 * BLK : 2 * BLK + INFO, start : start + LANES] = info


def pack(bucket, seg, keys, values):
    row_count, feature_count = keys.shape
    half_features = feature_count // HALVES
    vmem = pl.BlockSpec(memory_space=pltpu.VMEM)
    return pl.pallas_call(
        pack_body,
        in_specs=[pl.BlockSpec(memory_space=pltpu.SMEM), vmem, vmem, vmem],
        out_specs=[vmem] * 3,
        out_shape=[
            jax.ShapeDtypeStruct((2 * row_count + INFO, feature_count), BF16),
            jax.ShapeDtypeStruct((2 * row_count + INFO, half_features), BF16),
            jax.ShapeDtypeStruct((2 * row_count, half_features), BF16),
        ],
        compiler_params=pltpu.CompilerParams(vmem_limit_bytes=VMEM_LIMIT),
        name="pack",
    )(bucket, seg, keys, values)


def after(value, *earlier):
    return lax.optimization_barrier((value, *earlier))[0]


def double(block, axis, mask):
    return jnp.concatenate([block, from_partner(block, axis, mask)], axis=0)


def local(queries, keys, values, d_out, segment_ids, block_bucket, block_mask, bias_table):
    level_count = lax.axis_size("seq").bit_length() - 1
    rows = [queries[0], d_out[0], keys[0], values[0]]
    scalars = (block_mask.reshape(-1), block_bucket.reshape(-1), segment_ids)
    table_rows = bias_table.reshape(H * NB, NB)
    far_levels = list(range(1, level_count))
    last = far_levels[-2:]

    def send(value, level):
        return from_partner(value, "seq", 1 << level)

    whole, first, second = pack(scalars[1], segment_ids, rows[2], rows[3])
    far = [{}, {}]
    for level in reversed(far_levels):
        far[0][level] = send(first, level)
    near = send(whole, 0)
    for level in reversed(far_levels):
        far[1][level] = send(after(second, near if level in last else far[0][level]), level)
    near_list = [near]
    near_count = len(near_list)

    one = attention_half(
        0, scalars, table_rows, rows, near_list, [far[0][level] for level in far_levels], None
    )
    terms = one[3 + near_count : 3 + level_count]
    back_one = {level: send(terms[level - 1], level) for level in reversed(far_levels)}
    early = [back_one[level] for level in far_levels if level not in last]
    late = [back_one[level] for level in last]
    two = attention_half(
        1, scalars, table_rows, rows, near_list, [far[1][level] for level in far_levels], one
    )
    terms = two[3 + near_count : 3 + level_count]
    back_two = {level: send(terms[level - 1], level) for level in reversed(last)}
    block = double(after(two[3 + level_count], *early), "seq", 1)
    for level in far_levels:
        if level not in last:
            back_two[level] = send(after(terms[level - 1], *late), level)
    near_back = send(after(two[2], *late), 0)
    block = after(block, *late)
    mask = 1
    while mask < lax.axis_size("dp"):
        block = double(block, "dp", mask)
        mask *= 2
    for level in far_levels:
        if level not in last:
            block = double(block, "seq", 1 << level)
    block = after(block, near_back, *[back_two[level] for level in far_levels if level not in last])
    blocks = [block]
    for mask in (1 << last[0], 1 << last[1], (1 << last[0]) | (1 << last[1])):
        blocks.append(from_partner(block, "seq", mask))
    table_total = table_of(blocks, level_count + 1)
    d_keys, d_values = finish(
        [one[2 + near_count], two[2 + near_count]],
        [near_back],
        [back[level] for back in (back_one, back_two) for level in far_levels],
    )
    return (two[0][None], two[1][None], d_keys[None], d_values[None], table_total)


def solution(mesh):
    rows = P("dp", "seq", None)
    in_specs = (
        rows,
        rows,
        rows,
        rows,
        P("dp", "seq"),
        P("dp", "seq"),
        P("dp", "seq", None, None),
        P(),
    )
    return jax.shard_map(
        local, mesh=mesh, in_specs=in_specs, out_specs=(rows,) * 4 + (P(),), check_vma=False
    )
```

```python
import functools

import jax
import jax.numpy as jnp
from jax import lax
from jax.experimental import pallas as pl
from jax.experimental.pallas import tpu as pltpu
from jax.sharding import PartitionSpec as P

H = 16
DH = 64
NB = 64
BLK = 128
HALVES = 2
INFO = 8
LANES = 128
PAIR_LANES = 2 * DH
BUCKET_LANE = 112
MASKED = -1e30
UNROLL = 4
VMEM_LIMIT = 16 * 2**20
FLOPS = 2 * 10**10

F32 = jnp.float32
BF16 = jnp.bfloat16


def contract(a, b, dim_a, dim_b):
    return lax.dot_general(a, b, (((dim_a,), (dim_b,)), ((), ())), preferred_element_type=F32)


def from_partner(value, axis, mask):
    pairs = [(source, source ^ mask) for source in range(lax.axis_size(axis))]
    return lax.ppermute(value, axis, pairs)


def lane_iota(shape):
    return lax.broadcasted_iota(jnp.int32, shape, len(shape) - 1)


def row_iota(shape):
    return lax.broadcasted_iota(jnp.int32, shape, len(shape) - 2)


def split_pair(pair, low):
    zero = jnp.zeros_like(pair)
    return jnp.concatenate([jnp.where(low, pair, zero), jnp.where(low, zero, pair)], axis=0)


def attention_body(near_count, far_count, half, *refs):
    section_count = 1 + near_count + far_count
    first = half == 0
    refs = list(refs)

    def take(count):
        taken, refs[:] = refs[:count], refs[count:]
        return taken

    seg_ref, param_ref, table_ref, q_ref, do_ref, own_pack_ref = take(6)
    near_refs = take(near_count)
    far_refs = take(far_count)
    if not first:
        masks, biases, pay_in_ref = take(3)
        earlier = take(2)
    out_ref, dq_ref = take(2)
    own_ref, *term_refs, pay_ref = take(1 + section_count)
    if first:
        masks, biases = take(2)
    half_features = far_refs[0].shape[1]
    half_heads = half_features // DH

    if first:
        own_bucket = param_ref[INFO : INFO + 1, :]
        seg_rows = seg_ref[...].astype(F32)
        in_row = row_iota((H, NB, LANES)).astype(F32) == own_bucket
        pay = jnp.zeros((1, LANES), F32)
        for s in range(section_count):
            if s == 0:
                seg_cols = seg_rows
                bucket = own_bucket
            else:
                source = near_refs[s - 1] if s <= near_count else far_refs[s - 1 - near_count]
                info = source[2 * BLK : 2 * BLK + INFO, 0:LANES].astype(F32)
                seg_cols = info[0:1]
                bucket = info[1:2]
            cols = jnp.broadcast_to(seg_cols, (BLK, BLK)).T
            masks[s * BLK : (s + 1) * BLK, :] = jnp.where(
                cols == seg_rows, jnp.broadcast_to(param_ref[s : s + 1, :], (BLK, BLK)), MASKED
            )
            hot = (row_iota((NB, LANES)).astype(F32) == bucket).astype(BF16)
            picked = contract(table_ref[...], hot, 1, 0).reshape(H, NB, LANES)
            biases[s] = jnp.sum(jnp.where(in_row, picked, 0.0), axis=1)
            pay = jnp.where(lane_iota(pay.shape) == BUCKET_LANE + s, bucket, pay)
        pay_ref[0] = pay
    else:
        pay_ref[0] = pay_in_ref[0]
        for source, target in zip(earlier, [out_ref, dq_ref]):
            target[:, 0 : half * half_features] = source[...]

    low = lane_iota((BLK, PAIR_LANES)) < DH
    lanes = lane_iota((1, LANES))

    def one_pair(pair, carry):
        here = pl.ds(pl.multiple_of(pair * PAIR_LANES, PAIR_LANES), PAIR_LANES)
        there = pl.ds(
            pl.multiple_of(half * half_features + pair * PAIR_LANES, PAIR_LANES), PAIR_LANES
        )
        mine = here if first else there
        head = half * half_heads + 2 * pair
        q_stack = split_pair(q_ref[:, there] * jnp.asarray(0.125, BF16), low)
        grad_stack = split_pair(do_ref[:, there], low)
        key_rows = jnp.concatenate(
            [own_pack_ref[0:BLK, there]]
            + [r[0:BLK, there] for r in near_refs]
            + [r[0:BLK, here] for r in far_refs],
            axis=0,
        )
        value_rows = jnp.concatenate(
            [own_pack_ref[BLK : 2 * BLK, there]]
            + [r[BLK : 2 * BLK, there] for r in near_refs]
            + [r[BLK : 2 * BLK, here] for r in far_refs],
            axis=0,
        )
        raw = contract(key_rows, q_stack, 1, 1)
        dprob = contract(value_rows, grad_stack, 1, 1)
        scores = []
        shifts = []
        top = None
        for s in range(section_count):
            block = slice(s * BLK, (s + 1) * BLK)
            mask = masks[block, :]
            score = raw[block] + jnp.concatenate([mask, mask], axis=1)
            bias = jnp.concatenate(
                [biases[s, pl.ds(head, 1), :], biases[s, pl.ds(head + 1, 1), :]], axis=1
            )
            best = jnp.max(score, axis=0, keepdims=True) + bias
            top = best if top is None else jnp.maximum(top, best)
            scores.append(score)
            shifts.append(bias)
        weights = [jnp.exp(scores[s] - (top - shifts[s])) for s in range(section_count)]
        total = sum(jnp.sum(weight, axis=0, keepdims=True) for weight in weights)
        inverse = 1.0 / total
        probs = [weight * inverse for weight in weights]
        probs_low = jnp.concatenate([prob.astype(BF16) for prob in probs], axis=0)
        out_stack = contract(probs_low, value_rows, 0, 0)
        pulls = [probs[s] * dprob[s * BLK : (s + 1) * BLK] for s in range(section_count)]
        delta = sum(jnp.sum(pull, axis=0, keepdims=True) for pull in pulls)
        dscores = [pulls[s] - probs[s] * delta for s in range(section_count)]
        dscore_low = jnp.concatenate([dscore.astype(BF16) for dscore in dscores], axis=0)
        value_terms = contract(probs_low, grad_stack, 1, 0)
        key_terms = contract(dscore_low, q_stack, 1, 0)
        dq_stack = contract(dscore_low, key_rows, 0, 0)
        out_ref[:, mine] = jnp.where(low, out_stack[:BLK], out_stack[BLK:]).astype(BF16)
        dq_ref[:, mine] = (jnp.where(low, dq_stack[:BLK], dq_stack[BLK:]) * 0.125).astype(BF16)
        pay = pay_ref[0]
        for s in range(section_count):
            sums = jnp.sum(dscores[s], axis=0, keepdims=True)
            even = jnp.sum(sums[:, :BLK], axis=1, keepdims=True)
            odd = jnp.sum(sums[:, BLK:], axis=1, keepdims=True)
            pay = jnp.where(lanes == s * H + head, even, pay)
            pay = jnp.where(lanes == s * H + head + 1, odd, pay)
            key_term = key_terms[s * BLK : (s + 1) * BLK]
            value_term = value_terms[s * BLK : (s + 1) * BLK]
            if s == 0:
                own_ref[0:BLK, here] = key_term
                own_ref[BLK : 2 * BLK, here] = value_term
            else:
                term_refs[s - 1][0:BLK, here] = key_term.astype(BF16)
                term_refs[s - 1][BLK : 2 * BLK, here] = value_term.astype(BF16)
        pay_ref[...] = jnp.broadcast_to(pay[:, None, :], pay_ref.shape)
        return carry

    lax.fori_loop(0, half_features // PAIR_LANES, one_pair, 0, unroll=UNROLL)


def attention_half(half, copies, scalars, table_rows, rows, near, far, previous):
    near_count, far_count = len(near), len(far)
    section_count = 1 + near_count + far_count
    row_count, feature_count = rows[0].shape
    half_features = feature_count // HALVES
    half_heads = half_features // DH
    vmem = pl.BlockSpec(memory_space=pltpu.VMEM)
    operands = [*scalars, table_rows, *rows, *near, *far]
    in_specs = [vmem] * len(operands)
    covered = (half + 1) * half_features
    packed = jax.ShapeDtypeStruct((2 * row_count, half_features), BF16)
    out_shape = [
        *[jax.ShapeDtypeStruct((row_count, covered), BF16)] * 2,
        jax.ShapeDtypeStruct((2 * row_count, half_features), F32),
        *[packed] * (section_count - 1),
        jax.ShapeDtypeStruct((1 if previous is None else copies, 1, LANES), F32),
    ]
    if previous is None:
        out_shape += [
            jax.ShapeDtypeStruct((section_count * BLK, BLK), F32),
            jax.ShapeDtypeStruct((section_count, H, LANES), F32),
        ]
    else:
        operands += [*previous[-2:], previous[-3], *previous[:2]]
        in_specs += [vmem] * 5
    return pl.pallas_call(
        functools.partial(attention_body, near_count, far_count, half),
        in_specs=in_specs,
        out_specs=[vmem] * len(out_shape),
        out_shape=out_shape,
        compiler_params=pltpu.CompilerParams(vmem_limit_bytes=VMEM_LIMIT),
        cost_estimate=pl.CostEstimate(
            flops=FLOPS, bytes_accessed=4 * 2**20, transcendentals=section_count * half_heads * BLK * BLK
        ),
        name="attention",
    )(*operands)


def gather_body(*refs):
    total = refs[0][...]
    for ref in refs[1:-1]:
        total = total + ref[...].astype(F32)
    refs[-1][...] = total


def gather_terms(own, terms):
    vmem = pl.BlockSpec(memory_space=pltpu.VMEM)
    return pl.pallas_call(
        gather_body,
        in_specs=[vmem] * (1 + len(terms)),
        out_specs=vmem,
        out_shape=jax.ShapeDtypeStruct(own.shape, F32),
        compiler_params=pltpu.CompilerParams(vmem_limit_bytes=VMEM_LIMIT),
        cost_estimate=pl.CostEstimate(flops=2**19, bytes_accessed=2**21, transcendentals=0),
        name="gather",
    )(own, *terms)


def finish_body(*refs):
    one_ref, two_ref, *term_refs = refs[:-2]
    half_features = one_ref.shape[1]
    for out_ref, block in zip(refs[-2:], (slice(0, BLK), slice(BLK, 2 * BLK))):
        out_ref[:, :half_features] = one_ref[block, :].astype(BF16)
        total = two_ref[block, :]
        for ref in term_refs:
            total = total + ref[block, :].astype(F32)
        out_ref[:, half_features:] = total.astype(BF16)


def finish(one, two, terms):
    vmem = pl.BlockSpec(memory_space=pltpu.VMEM)
    out = jax.ShapeDtypeStruct((one.shape[0] // 2, HALVES * one.shape[1]), BF16)
    return pl.pallas_call(
        finish_body,
        in_specs=[vmem] * (2 + len(terms)),
        out_specs=[vmem, vmem],
        out_shape=[out, out],
        compiler_params=pltpu.CompilerParams(vmem_limit_bytes=VMEM_LIMIT),
        cost_estimate=pl.CostEstimate(flops=2**19, bytes_accessed=2**21, transcendentals=0),
        name="finish",
    )(one, two, *terms)


def table_body(section_count, *refs):
    table_ref = refs[1]
    gathered_ref, scratch = refs[0], refs[2]
    count = gathered_ref.shape[0]

    def copy_row(row, carry):
        scratch[pl.ds(row, 1), :] = gathered_ref[row]
        return carry

    lax.fori_loop(0, count, copy_row, 0, unroll=8)
    gathered = scratch[...]
    lanes = lane_iota((count, PAIR_LANES))
    column = jnp.where(lanes < NB, lanes, lanes - NB).astype(F32)
    bucket = gathered[:, BUCKET_LANE : BUCKET_LANE + 1]
    row_hot = (lane_iota((count, NB)).astype(F32) == bucket).astype(F32)
    rows = jnp.concatenate([row_hot] * section_count, axis=0)
    hots = [
        column == gathered[:, BUCKET_LANE + s : BUCKET_LANE + s + 1] for s in range(section_count)
    ]
    for pair in range(H // 2):
        parts = []
        for s in range(section_count):
            lane = s * H + 2 * pair
            value = jnp.where(lanes < NB, gathered[:, lane : lane + 1], gathered[:, lane + 1 : lane + 2])
            parts.append(jnp.where(hots[s], value, 0.0))
        tile = lax.dot_general(
            rows,
            jnp.concatenate(parts, axis=0),
            (((0,), (0,)), ((), ())),
            preferred_element_type=F32,
            precision=lax.Precision.HIGHEST,
        )
        table_ref[2 * pair] = tile[:, :NB]
        table_ref[2 * pair + 1] = tile[:, NB:]


def table_of(gathered, section_count):
    vmem = pl.BlockSpec(memory_space=pltpu.VMEM)
    return pl.pallas_call(
        functools.partial(table_body, section_count),
        in_specs=[vmem],
        out_specs=vmem,
        out_shape=jax.ShapeDtypeStruct((H, NB, NB), F32),
        scratch_shapes=[pltpu.VMEM((gathered.shape[0], LANES), F32)],
        compiler_params=pltpu.CompilerParams(vmem_limit_bytes=VMEM_LIMIT),
        name="table",
    )(gathered)


def in_hbm(array):
    return pltpu.with_memory_space_constraint(array, pltpu.HBM)


def pack_body(*refs):
    mask_hbm, bucket_hbm, seg_hbm, key_hbm, value_hbm = refs[:5]
    whole_ref, first_ref, second_ref, seg_ref, param_ref = refs[5:10]
    mask_ref, bucket_ref, sems = refs[10:]
    half_features = first_ref.shape[1]
    small = [(mask_hbm, mask_ref), (bucket_hbm, bucket_ref), (seg_hbm, seg_ref)]
    copies = [
        pltpu.make_async_copy(source, target, sems.at[i]) for i, (source, target) in enumerate(small)
    ]
    for target, start, width in (
        (first_ref, 0, half_features),
        (second_ref, half_features, half_features),
        (whole_ref, 0, HALVES * half_features),
    ):
        for row, source in ((0, key_hbm), (BLK, value_hbm)):
            copies.append(
                pltpu.make_async_copy(
                    source.at[:, pl.ds(start, width)],
                    target.at[pl.ds(row, BLK), :],
                    sems.at[len(copies)],
                )
            )
    for copy in copies:
        copy.start()
    for copy in copies[: len(small)]:
        copy.wait()
    top = row_iota((INFO, LANES)) == 0
    bucket = jnp.broadcast_to(bucket_ref[...], (INFO, LANES))
    info = jnp.where(top, seg_ref[...], bucket).astype(F32).astype(BF16)
    for target in (whole_ref, first_ref):
        for start in range(0, target.shape[1], LANES):
            target[2 * BLK : 2 * BLK + INFO, start : start + LANES] = info
    lines = row_iota((2 * INFO, LANES))
    params = jnp.where(lines == INFO, bucket_ref[...].astype(F32), 0.0)
    for s in range(1, mask_ref.shape[1]):
        shut = jnp.where(mask_ref[:, s : s + 1] != 0, 0.0, MASKED)
        params = jnp.where(lines == s, shut, params)
    param_ref[...] = params
    for copy in copies[len(small) :]:
        copy.wait()


def pack(mask, bucket, seg, keys, values):
    row_count, feature_count = keys.shape
    half_features = feature_count // HALVES
    vmem = pl.BlockSpec(memory_space=pltpu.VMEM)
    hbm = pl.BlockSpec(memory_space=pltpu.HBM)
    return pl.pallas_call(
        pack_body,
        in_specs=[hbm, pl.BlockSpec(memory_space=pl.ANY), hbm, hbm, hbm],
        out_specs=[vmem] * 5,
        out_shape=[
            jax.ShapeDtypeStruct((2 * row_count + INFO, feature_count), BF16),
            jax.ShapeDtypeStruct((2 * row_count + INFO, half_features), BF16),
            jax.ShapeDtypeStruct((2 * row_count, half_features), BF16),
            jax.ShapeDtypeStruct(seg.shape, jnp.int32),
            jax.ShapeDtypeStruct((2 * INFO, LANES), F32),
        ],
        scratch_shapes=[
            pltpu.VMEM(mask.shape, jnp.int32),
            pltpu.VMEM(bucket.shape, jnp.int32),
            pltpu.SemaphoreType.DMA((3 + 3 * HALVES,)),
        ],
        compiler_params=pltpu.CompilerParams(vmem_limit_bytes=VMEM_LIMIT),
        name="pack",
    )(*[bucket if a is bucket else in_hbm(a) for a in (mask, bucket, seg, keys, values)])


def load_body(*refs):
    count = len(refs) // 2
    sems = refs[-1]
    copies = [
        pltpu.make_async_copy(source, target, sems.at[i])
        for i, (source, target) in enumerate(zip(refs[:count], refs[count : 2 * count]))
    ]
    for copy in copies:
        copy.start()
    for copy in copies:
        copy.wait()


def load(*arrays):
    return pl.pallas_call(
        load_body,
        in_specs=[pl.BlockSpec(memory_space=pltpu.HBM)] * len(arrays),
        out_specs=[pl.BlockSpec(memory_space=pltpu.VMEM)] * len(arrays),
        out_shape=[jax.ShapeDtypeStruct(a.shape, a.dtype) for a in arrays],
        scratch_shapes=[pltpu.SemaphoreType.DMA((len(arrays),))],
        compiler_params=pltpu.CompilerParams(vmem_limit_bytes=VMEM_LIMIT),
        name="load",
    )(*[in_hbm(a) for a in arrays])


def after(value, *earlier):
    return lax.optimization_barrier((value, *earlier))[0]


def double(block, axis, mask):
    return jnp.concatenate([block, from_partner(block, axis, mask)], axis=0)


def local(queries, keys, values, d_out, segment_ids, block_bucket, block_mask, bias_table):
    level_count = lax.axis_size("seq").bit_length() - 1
    far_levels = list(range(1, level_count))
    last = far_levels[-2:]

    def send(value, level):
        return from_partner(value, "seq", 1 << level)

    whole, first, second, *scalars = pack(
        block_mask.reshape(1, -1), block_bucket, segment_ids, keys[0], values[0]
    )
    query_rows, grad_rows, table_rows = load(queries[0], d_out[0], bias_table.reshape(H * NB, NB))
    rows = [query_rows, grad_rows, whole]
    far = [{}, {}]
    near = send(whole, 0)
    for level in reversed(far_levels):
        far[0][level] = send(first, level)
    for level in far_levels:
        gate = (near, query_rows)
        far[1][level] = send(after(second, *gate), level)
    near_list = [near]
    near_count = len(near_list)

    device_count = lax.axis_size("dp") * lax.axis_size("seq")
    one = attention_half(
        0, device_count, scalars, table_rows, rows, near_list, [far[0][level] for level in far_levels], None
    )
    middle = [level for level in range(level_count) if level not in last]
    terms = one[3 : 3 + level_count]
    back_one = {level: send(terms[level], level) for level in [*last, *middle]}
    late = [back_one[level] for level in last]
    two = attention_half(
        1, device_count, scalars, table_rows, rows, near_list, [far[1][level] for level in far_levels], one
    )
    terms = two[3 : 3 + level_count]
    back_two = {level: send(terms[level], level) for level in last}
    block = after(two[3 + level_count], *[back_one[level] for level in middle])
    gathered = lax.all_to_all(block, ("dp", "seq"), 0, 0, tiled=True)
    for level in middle:
        back_two[level] = send(after(terms[level], *late), level)
    sum_one = gather_terms(one[2], list(back_one.values()))
    sum_two = gather_terms(two[2], [back_two[level] for level in last])
    d_keys, d_values = finish(sum_one, sum_two, [back_two[level] for level in middle])
    table_total = table_of(after(gathered, d_keys), level_count + 1)
    return (two[0][None], two[1][None], d_keys[None], d_values[None], table_total)


def solution(mesh):
    rows = P("dp", "seq", None)
    in_specs = (
        rows,
        rows,
        rows,
        rows,
        P("dp", "seq"),
        P("dp", "seq"),
        P("dp", "seq", None, None),
        P(),
    )
    return jax.shard_map(
        local, mesh=mesh, in_specs=in_specs, out_specs=(rows,) * 4 + (P(),), check_vma=False
    )
```

```python
import functools

import jax
import jax.numpy as jnp
from jax import lax
from jax.experimental import pallas as pl
from jax.experimental.pallas import tpu as pltpu
from jax.sharding import PartitionSpec as P

H = 16
DH = 64
NB = 64
BLK = 128
HALVES = 2
INFO = 8
LANES = 128
PAIR_LANES = 2 * DH
BUCKET_LANE = 112
MASKED = -1e30
TABLE_ROWS = 32
UNROLL = 4
VMEM_LIMIT = 16 * 2**20
FLOPS = 2 * 10**10

F32 = jnp.float32
BF16 = jnp.bfloat16


def contract(a, b, dim_a, dim_b):
    return lax.dot_general(a, b, (((dim_a,), (dim_b,)), ((), ())), preferred_element_type=F32)


def from_partner(value, axis, mask):
    pairs = [(source, source ^ mask) for source in range(lax.axis_size(axis))]
    return lax.ppermute(value, axis, pairs)


def lane_iota(shape):
    return lax.broadcasted_iota(jnp.int32, shape, len(shape) - 1)


def row_iota(shape):
    return lax.broadcasted_iota(jnp.int32, shape, len(shape) - 2)


def split_pair(pair, low):
    zero = jnp.zeros_like(pair)
    return jnp.concatenate([jnp.where(low, pair, zero), jnp.where(low, zero, pair)], axis=0)


def attention_body(near_count, far_count, half, *refs):
    section_count = 1 + near_count + far_count
    first = half == 0
    refs = list(refs)

    def take(count):
        taken, refs[:] = refs[:count], refs[count:]
        return taken

    seg_ref, param_ref, table_ref, q_ref, do_ref, own_pack_ref = take(6)
    near_refs = take(near_count)
    far_refs = take(far_count)
    if not first:
        masks, biases, pay_in_ref = take(3)
        earlier = take(2)
    out_ref, dq_ref = take(2)
    own_ref, *term_refs, pay_ref = take(1 + section_count)
    if first:
        masks, biases = take(2)
    half_features = far_refs[0].shape[1]
    half_heads = half_features // DH

    if first:
        own_bucket = param_ref[INFO : INFO + 1, :]
        seg_rows = seg_ref[...].astype(F32)
        in_row = row_iota((H, NB, LANES)).astype(F32) == own_bucket
        pay = jnp.zeros((1, LANES), F32)
        for s in range(section_count):
            if s == 0:
                seg_cols = seg_rows
                bucket = own_bucket
            else:
                source = near_refs[s - 1] if s <= near_count else far_refs[s - 1 - near_count]
                info = source[2 * BLK : 2 * BLK + INFO, 0:LANES].astype(F32)
                seg_cols = info[0:1]
                bucket = info[1:2]
            cols = jnp.broadcast_to(seg_cols, (BLK, BLK)).T
            masks[s * BLK : (s + 1) * BLK, :] = jnp.where(
                cols == seg_rows, jnp.broadcast_to(param_ref[s : s + 1, :], (BLK, BLK)), MASKED
            )
            hot = (row_iota((NB, LANES)).astype(F32) == bucket).astype(BF16)
            picked = contract(table_ref[...], hot, 1, 0).reshape(H, NB, LANES)
            biases[s] = jnp.sum(jnp.where(in_row, picked, 0.0), axis=1)
            pay = jnp.where(lane_iota(pay.shape) == BUCKET_LANE + s, bucket, pay)
        pay_ref[0] = pay
    else:
        pay_ref[0] = pay_in_ref[0]
        for source, target in zip(earlier, [out_ref, dq_ref]):
            target[:, 0 : half * half_features] = source[...]

    low = lane_iota((BLK, PAIR_LANES)) < DH
    lanes = lane_iota((1, LANES))

    def one_pair(pair, carry):
        here = pl.ds(pl.multiple_of(pair * PAIR_LANES, PAIR_LANES), PAIR_LANES)
        there = pl.ds(
            pl.multiple_of(half * half_features + pair * PAIR_LANES, PAIR_LANES), PAIR_LANES
        )
        mine = here if first else there
        head = half * half_heads + 2 * pair
        q_stack = split_pair(q_ref[:, there] * jnp.asarray(0.125, BF16), low)
        grad_stack = split_pair(do_ref[:, there], low)
        key_rows = jnp.concatenate(
            [own_pack_ref[0:BLK, there]]
            + [r[0:BLK, there] for r in near_refs]
            + [r[0:BLK, here] for r in far_refs],
            axis=0,
        )
        value_rows = jnp.concatenate(
            [own_pack_ref[BLK : 2 * BLK, there]]
            + [r[BLK : 2 * BLK, there] for r in near_refs]
            + [r[BLK : 2 * BLK, here] for r in far_refs],
            axis=0,
        )
        raw = contract(key_rows, q_stack, 1, 1)
        dprob = contract(value_rows, grad_stack, 1, 1)
        scores = []
        shifts = []
        top = None
        for s in range(section_count):
            block = slice(s * BLK, (s + 1) * BLK)
            mask = masks[block, :]
            score = raw[block] + jnp.concatenate([mask, mask], axis=1)
            bias = jnp.concatenate(
                [biases[s, pl.ds(head, 1), :], biases[s, pl.ds(head + 1, 1), :]], axis=1
            )
            best = jnp.max(score, axis=0, keepdims=True) + bias
            top = best if top is None else jnp.maximum(top, best)
            scores.append(score)
            shifts.append(bias)
        weights = [jnp.exp(scores[s] - (top - shifts[s])) for s in range(section_count)]
        total = sum(jnp.sum(weight, axis=0, keepdims=True) for weight in weights)
        inverse = 1.0 / total
        probs = [weight * inverse for weight in weights]
        probs_low = jnp.concatenate([prob.astype(BF16) for prob in probs], axis=0)
        out_stack = contract(probs_low, value_rows, 0, 0)
        pulls = [probs[s] * dprob[s * BLK : (s + 1) * BLK] for s in range(section_count)]
        delta = sum(jnp.sum(pull, axis=0, keepdims=True) for pull in pulls)
        dscores = [pulls[s] - probs[s] * delta for s in range(section_count)]
        dscore_low = jnp.concatenate([dscore.astype(BF16) for dscore in dscores], axis=0)
        value_terms = contract(probs_low, grad_stack, 1, 0)
        key_terms = contract(dscore_low, q_stack, 1, 0)
        dq_stack = contract(dscore_low, key_rows, 0, 0)
        out_ref[:, mine] = jnp.where(low, out_stack[:BLK], out_stack[BLK:]).astype(BF16)
        dq_ref[:, mine] = (jnp.where(low, dq_stack[:BLK], dq_stack[BLK:]) * 0.125).astype(BF16)
        pay = pay_ref[0]
        for s in range(section_count):
            sums = jnp.sum(dscores[s], axis=0, keepdims=True)
            even = jnp.sum(sums[:, :BLK], axis=1, keepdims=True)
            odd = jnp.sum(sums[:, BLK:], axis=1, keepdims=True)
            pay = jnp.where(lanes == s * H + head, even, pay)
            pay = jnp.where(lanes == s * H + head + 1, odd, pay)
            key_term = key_terms[s * BLK : (s + 1) * BLK]
            value_term = value_terms[s * BLK : (s + 1) * BLK]
            if s == 0:
                own_ref[0:BLK, here] = key_term
                own_ref[BLK : 2 * BLK, here] = value_term
            else:
                term_refs[s - 1][0:BLK, here] = key_term.astype(BF16)
                term_refs[s - 1][BLK : 2 * BLK, here] = value_term.astype(BF16)
        pay_ref[...] = jnp.broadcast_to(pay[:, None, :], pay_ref.shape)
        return carry

    lax.fori_loop(0, half_features // PAIR_LANES, one_pair, 0, unroll=UNROLL)


def attention_half(half, copies, scalars, table_rows, rows, near, far, previous):
    near_count, far_count = len(near), len(far)
    section_count = 1 + near_count + far_count
    row_count, feature_count = rows[0].shape
    half_features = feature_count // HALVES
    half_heads = half_features // DH
    vmem = pl.BlockSpec(memory_space=pltpu.VMEM)
    operands = [*scalars, table_rows, *rows, *near, *far]
    in_specs = [vmem] * len(operands)
    covered = (half + 1) * half_features
    packed = jax.ShapeDtypeStruct((2 * row_count, half_features), BF16)
    out_shape = [
        *[jax.ShapeDtypeStruct((row_count, covered), BF16)] * 2,
        jax.ShapeDtypeStruct((2 * row_count, half_features), F32),
        *[packed] * (section_count - 1),
        jax.ShapeDtypeStruct((1 if previous is None else copies, 1, LANES), F32),
    ]
    if previous is None:
        out_shape += [
            jax.ShapeDtypeStruct((section_count * BLK, BLK), F32),
            jax.ShapeDtypeStruct((section_count, H, LANES), F32),
        ]
    else:
        operands += [*previous[-2:], previous[-3], *previous[:2]]
        in_specs += [vmem] * 5
    return pl.pallas_call(
        functools.partial(attention_body, near_count, far_count, half),
        in_specs=in_specs,
        out_specs=[vmem] * len(out_shape),
        out_shape=out_shape,
        compiler_params=pltpu.CompilerParams(vmem_limit_bytes=VMEM_LIMIT),
        cost_estimate=pl.CostEstimate(
            flops=FLOPS, bytes_accessed=4 * 2**20, transcendentals=section_count * half_heads * BLK * BLK
        ),
        name="attention",
    )(*operands)


def gather_body(*refs):
    total = refs[0][...]
    for ref in refs[1:-1]:
        total = total + ref[...].astype(F32)
    refs[-1][...] = total


def gather_terms(own, terms):
    vmem = pl.BlockSpec(memory_space=pltpu.VMEM)
    return pl.pallas_call(
        gather_body,
        in_specs=[vmem] * (1 + len(terms)),
        out_specs=vmem,
        out_shape=jax.ShapeDtypeStruct(own.shape, F32),
        compiler_params=pltpu.CompilerParams(vmem_limit_bytes=VMEM_LIMIT),
        cost_estimate=pl.CostEstimate(flops=2**19, bytes_accessed=2**21, transcendentals=0),
        name="gather",
    )(own, *terms)


def finish_body(*refs):
    one_ref, two_ref, *term_refs = refs[:-2]
    half_features = one_ref.shape[1]
    for out_ref, block in zip(refs[-2:], (slice(0, BLK), slice(BLK, 2 * BLK))):
        out_ref[:, :half_features] = one_ref[block, :].astype(BF16)
        total = two_ref[block, :]
        for ref in term_refs:
            total = total + ref[block, :].astype(F32)
        out_ref[:, half_features:] = total.astype(BF16)


def finish(one, two, terms):
    vmem = pl.BlockSpec(memory_space=pltpu.VMEM)
    out = jax.ShapeDtypeStruct((one.shape[0] // 2, HALVES * one.shape[1]), BF16)
    return pl.pallas_call(
        finish_body,
        in_specs=[vmem] * (2 + len(terms)),
        out_specs=[vmem, vmem],
        out_shape=[out, out],
        compiler_params=pltpu.CompilerParams(vmem_limit_bytes=VMEM_LIMIT),
        cost_estimate=pl.CostEstimate(flops=2**19, bytes_accessed=2**21, transcendentals=0),
        name="finish",
    )(one, two, *terms)


def table_part(section_count, gathered):
    count = gathered.shape[0]
    lanes = lane_iota((count, LANES))
    column = jnp.where(lanes < NB, lanes, lanes - NB).astype(F32)
    section = jnp.right_shift(lanes, 4)
    high = gathered.astype(BF16)
    low = (gathered - high.astype(F32)).astype(BF16)
    row_hot = (lane_iota((count, NB)).astype(F32) == gathered[:, BUCKET_LANE : BUCKET_LANE + 1]).astype(BF16)
    spread = jnp.bitwise_and(row_iota((LANES, H * NB)), H - 1) == jnp.right_shift(
        lane_iota((LANES, H * NB)), 6
    )
    spread = jnp.where(spread, 1.0, 0.0).astype(BF16)
    pieces = []
    for s in range(section_count):
        for part in (high, low):
            pieces.append(jnp.where(section == s, part, jnp.zeros_like(part)))
    wide = contract(jnp.concatenate(pieces, axis=0), spread, 1, 0)
    masked = []
    for s in range(section_count):
        hot = column == gathered[:, BUCKET_LANE + s : BUCKET_LANE + s + 1]
        hot = jnp.concatenate([hot.astype(F32)] * (H * NB // LANES), axis=1)
        for part in range(2):
            start = (2 * s + part) * count
            masked.append((wide[start : start + count] * hot).astype(BF16))
    rows = jnp.concatenate([row_hot] * (2 * section_count), axis=0)
    return contract(rows, jnp.concatenate(masked, axis=0), 0, 0)


def table_body(section_count, gathered_ref, table_ref, scratch, total):
    count = gathered_ref.shape[0]

    def copy_row(row, carry):
        scratch[pl.ds(row, 1), :] = gathered_ref[row]
        return carry

    lax.fori_loop(0, count, copy_row, 0, unroll=8)
    if count <= TABLE_ROWS:
        table = table_part(section_count, scratch[...])
    else:
        total[...] = jnp.zeros_like(total)

        def add_part(step, carry):
            start = pl.multiple_of(step * TABLE_ROWS, TABLE_ROWS)
            total[...] += table_part(section_count, scratch[pl.ds(start, TABLE_ROWS), :])
            return carry

        lax.fori_loop(0, count // TABLE_ROWS, add_part, 0)
        table = total[...]
    for head in range(H):
        table_ref[head] = table[:, head * NB : (head + 1) * NB]


def table_of(gathered, section_count):
    vmem = pl.BlockSpec(memory_space=pltpu.VMEM)
    return pl.pallas_call(
        functools.partial(table_body, section_count),
        in_specs=[vmem],
        out_specs=vmem,
        out_shape=jax.ShapeDtypeStruct((H, NB, NB), F32),
        scratch_shapes=[
            pltpu.VMEM((gathered.shape[0], LANES), F32),
            pltpu.VMEM((NB, H * NB), F32),
        ],
        compiler_params=pltpu.CompilerParams(vmem_limit_bytes=VMEM_LIMIT),
        name="table",
    )(gathered)


def in_hbm(array):
    return pltpu.with_memory_space_constraint(array, pltpu.HBM)


def pack_body(*refs):
    mask_hbm, bucket_hbm, seg_hbm, key_hbm, value_hbm = refs[:5]
    whole_ref, first_ref, second_ref, seg_ref, param_ref = refs[5:10]
    mask_ref, bucket_ref, sems = refs[10:]
    half_features = first_ref.shape[1]
    small = [(mask_hbm, mask_ref), (bucket_hbm, bucket_ref), (seg_hbm, seg_ref)]
    copies = [
        pltpu.make_async_copy(source, target, sems.at[i]) for i, (source, target) in enumerate(small)
    ]
    for target, start, width in (
        (first_ref, 0, half_features),
        (second_ref, half_features, half_features),
        (whole_ref, 0, HALVES * half_features),
    ):
        for row, source in ((0, key_hbm), (BLK, value_hbm)):
            copies.append(
                pltpu.make_async_copy(
                    source.at[:, pl.ds(start, width)],
                    target.at[pl.ds(row, BLK), :],
                    sems.at[len(copies)],
                )
            )
    for copy in copies:
        copy.start()
    for copy in copies[: len(small)]:
        copy.wait()
    top = row_iota((INFO, LANES)) == 0
    bucket = jnp.broadcast_to(bucket_ref[...], (INFO, LANES))
    info = jnp.where(top, seg_ref[...], bucket).astype(F32).astype(BF16)
    for target in (whole_ref, first_ref):
        for start in range(0, target.shape[1], LANES):
            target[2 * BLK : 2 * BLK + INFO, start : start + LANES] = info
    lines = row_iota((2 * INFO, LANES))
    params = jnp.where(lines == INFO, bucket_ref[...].astype(F32), 0.0)
    for s in range(1, mask_ref.shape[1]):
        shut = jnp.where(mask_ref[:, s : s + 1] != 0, 0.0, MASKED)
        params = jnp.where(lines == s, shut, params)
    param_ref[...] = params
    for copy in copies[len(small) :]:
        copy.wait()


def pack(mask, bucket, seg, keys, values):
    row_count, feature_count = keys.shape
    half_features = feature_count // HALVES
    vmem = pl.BlockSpec(memory_space=pltpu.VMEM)
    hbm = pl.BlockSpec(memory_space=pltpu.HBM)
    return pl.pallas_call(
        pack_body,
        in_specs=[hbm, pl.BlockSpec(memory_space=pl.ANY), hbm, hbm, hbm],
        out_specs=[vmem] * 5,
        out_shape=[
            jax.ShapeDtypeStruct((2 * row_count + INFO, feature_count), BF16),
            jax.ShapeDtypeStruct((2 * row_count + INFO, half_features), BF16),
            jax.ShapeDtypeStruct((2 * row_count, half_features), BF16),
            jax.ShapeDtypeStruct(seg.shape, jnp.int32),
            jax.ShapeDtypeStruct((2 * INFO, LANES), F32),
        ],
        scratch_shapes=[
            pltpu.VMEM(mask.shape, jnp.int32),
            pltpu.VMEM(bucket.shape, jnp.int32),
            pltpu.SemaphoreType.DMA((3 + 3 * HALVES,)),
        ],
        compiler_params=pltpu.CompilerParams(vmem_limit_bytes=VMEM_LIMIT),
        name="pack",
    )(*[bucket if a is bucket else in_hbm(a) for a in (mask, bucket, seg, keys, values)])


def load_body(*refs):
    count = len(refs) // 2
    sems = refs[-1]
    copies = [
        pltpu.make_async_copy(source, target, sems.at[i])
        for i, (source, target) in enumerate(zip(refs[:count], refs[count : 2 * count]))
    ]
    for copy in copies:
        copy.start()
    for copy in copies:
        copy.wait()


def load(*arrays):
    return pl.pallas_call(
        load_body,
        in_specs=[pl.BlockSpec(memory_space=pltpu.HBM)] * len(arrays),
        out_specs=[pl.BlockSpec(memory_space=pltpu.VMEM)] * len(arrays),
        out_shape=[jax.ShapeDtypeStruct(a.shape, a.dtype) for a in arrays],
        scratch_shapes=[pltpu.SemaphoreType.DMA((len(arrays),))],
        compiler_params=pltpu.CompilerParams(vmem_limit_bytes=VMEM_LIMIT),
        name="load",
    )(*[in_hbm(a) for a in arrays])


def after(value, *earlier):
    return lax.optimization_barrier((value, *earlier))[0]


def double(block, axis, mask):
    return jnp.concatenate([block, from_partner(block, axis, mask)], axis=0)


def local(queries, keys, values, d_out, segment_ids, block_bucket, block_mask, bias_table):
    level_count = lax.axis_size("seq").bit_length() - 1
    far_levels = list(range(1, level_count))
    last = far_levels[-2:]

    def send(value, level):
        return from_partner(value, "seq", 1 << level)

    whole, first, second, *scalars = pack(
        block_mask.reshape(1, -1), block_bucket, segment_ids, keys[0], values[0]
    )
    query_rows, grad_rows, table_rows = load(queries[0], d_out[0], bias_table.reshape(H * NB, NB))
    rows = [query_rows, grad_rows, whole]
    far = [{}, {}]
    near = send(whole, 0)
    for level in reversed(far_levels):
        far[0][level] = send(first, level)
    for level in far_levels:
        gate = (near, query_rows)
        far[1][level] = send(after(second, *gate), level)
    near_list = [near]
    near_count = len(near_list)

    device_count = lax.axis_size("dp") * lax.axis_size("seq")
    one = attention_half(
        0, device_count, scalars, table_rows, rows, near_list, [far[0][level] for level in far_levels], None
    )
    middle = [level for level in range(level_count) if level not in last]
    terms = one[3 : 3 + level_count]
    back_one = {level: send(terms[level], level) for level in [*last, *middle[1:]]}
    late = [back_one[level] for level in last]
    two = attention_half(
        1, device_count, scalars, table_rows, rows, near_list, [far[1][level] for level in far_levels], one
    )
    terms = two[3 : 3 + level_count]
    back_two = {level: send(terms[level], level) for level in last}
    block = two[3 + level_count]
    gathered = lax.all_to_all(block, ("dp", "seq"), 0, 0, tiled=True)
    for level in middle:
        back_two[level] = send(after(terms[level], *late, *[back_one[m] for m in middle[1:]]), level)
    back_one[0] = send(after(one[3], *late), 0)
    sum_one = gather_terms(one[2], list(back_one.values()))
    sum_two = gather_terms(two[2], [back_two[level] for level in last])
    d_keys, d_values = finish(sum_one, sum_two, [back_two[level] for level in middle])
    table_total = table_of(after(gathered, d_keys), level_count + 1)
    return (two[0][None], two[1][None], d_keys[None], d_values[None], table_total)


def solution(mesh):
    rows = P("dp", "seq", None)
    in_specs = (
        rows,
        rows,
        rows,
        rows,
        P("dp", "seq"),
        P("dp", "seq"),
        P("dp", "seq", None, None),
        P(),
    )
    return jax.shard_map(
        local, mesh=mesh, in_specs=in_specs, out_specs=(rows,) * 4 + (P(),), check_vma=False
    )
```

```python
import functools

import jax
import jax.numpy as jnp
from jax import lax
from jax.experimental import pallas as pl
from jax.experimental.pallas import tpu as pltpu
from jax.sharding import PartitionSpec as P

H = 16
DH = 64
NB = 64
BLK = 128
HALVES = 2
INFO = 8
LANES = 128
PAIR_LANES = 2 * DH
BUCKET_LANE = 112
MASKED = -1e30
TABLE_ROWS = 32
UNROLL = 4
VMEM_LIMIT = 16 * 2**20
FLOPS = 2 * 10**10

F32 = jnp.float32
BF16 = jnp.bfloat16


def contract(a, b, dim_a, dim_b):
    return lax.dot_general(a, b, (((dim_a,), (dim_b,)), ((), ())), preferred_element_type=F32)


def from_partner(value, axis, mask):
    pairs = [(source, source ^ mask) for source in range(lax.axis_size(axis))]
    return lax.ppermute(value, axis, pairs)


def lane_iota(shape):
    return lax.broadcasted_iota(jnp.int32, shape, len(shape) - 1)


def row_iota(shape):
    return lax.broadcasted_iota(jnp.int32, shape, len(shape) - 2)


def split_pair(pair, low):
    zero = jnp.zeros_like(pair)
    return jnp.concatenate([jnp.where(low, pair, zero), jnp.where(low, zero, pair)], axis=0)


def attention_body(near_count, far_count, half, *refs):
    section_count = 1 + near_count + far_count
    first = half == 0
    refs = list(refs)

    def take(count):
        taken, refs[:] = refs[:count], refs[count:]
        return taken

    seg_ref, param_ref, table_ref, q_ref, do_ref, own_pack_ref = take(6)
    near_refs = take(near_count)
    far_refs = take(far_count)
    if not first:
        masks, biases, pay_in_ref = take(3)
        earlier = take(2)
    out_ref, dq_ref = take(2)
    own_ref, *term_refs, pay_ref = take(1 + section_count)
    if first:
        masks, biases = take(2)
    half_features = far_refs[0].shape[1]
    half_heads = half_features // DH

    if first:
        own_bucket = param_ref[INFO : INFO + 1, :]
        seg_rows = seg_ref[...].astype(F32)
        in_row = row_iota((H, NB, LANES)).astype(F32) == own_bucket
        pay = jnp.zeros((1, LANES), F32)
        for s in range(section_count):
            if s == 0:
                seg_cols = seg_rows
                bucket = own_bucket
            else:
                source = near_refs[s - 1] if s <= near_count else far_refs[s - 1 - near_count]
                info = source[2 * BLK : 2 * BLK + INFO, 0:LANES].astype(F32)
                seg_cols = info[0:1]
                bucket = info[1:2]
            cols = jnp.broadcast_to(seg_cols, (BLK, BLK)).T
            masks[s * BLK : (s + 1) * BLK, :] = jnp.where(
                cols == seg_rows, jnp.broadcast_to(param_ref[s : s + 1, :], (BLK, BLK)), MASKED
            )
            hot = (row_iota((NB, LANES)).astype(F32) == bucket).astype(BF16)
            picked = contract(table_ref[...], hot, 1, 0).reshape(H, NB, LANES)
            biases[s] = jnp.sum(jnp.where(in_row, picked, 0.0), axis=1)
            pay = jnp.where(lane_iota(pay.shape) == BUCKET_LANE + s, bucket, pay)
        pay_ref[0] = pay
    else:
        pay_ref[0] = pay_in_ref[0]
        for source, target in zip(earlier, [out_ref, dq_ref]):
            target[:, 0 : half * half_features] = source[...]

    low = lane_iota((BLK, PAIR_LANES)) < DH
    lanes = lane_iota((1, LANES))

    def one_pair(pair, carry):
        here = pl.ds(pl.multiple_of(pair * PAIR_LANES, PAIR_LANES), PAIR_LANES)
        there = pl.ds(
            pl.multiple_of(half * half_features + pair * PAIR_LANES, PAIR_LANES), PAIR_LANES
        )
        mine = here if first else there
        head = half * half_heads + 2 * pair
        q_stack = split_pair(q_ref[:, there] * jnp.asarray(0.125, BF16), low)
        grad_stack = split_pair(do_ref[:, there], low)
        key_rows = jnp.concatenate(
            [own_pack_ref[0:BLK, there]]
            + [r[0:BLK, there] for r in near_refs]
            + [r[0:BLK, here] for r in far_refs],
            axis=0,
        )
        value_rows = jnp.concatenate(
            [own_pack_ref[BLK : 2 * BLK, there]]
            + [r[BLK : 2 * BLK, there] for r in near_refs]
            + [r[BLK : 2 * BLK, here] for r in far_refs],
            axis=0,
        )
        raw = contract(key_rows, q_stack, 1, 1)
        dprob = contract(value_rows, grad_stack, 1, 1)
        scores = []
        shifts = []
        top = None
        for s in range(section_count):
            block = slice(s * BLK, (s + 1) * BLK)
            mask = masks[block, :]
            score = raw[block] + jnp.concatenate([mask, mask], axis=1)
            bias = jnp.concatenate(
                [biases[s, pl.ds(head, 1), :], biases[s, pl.ds(head + 1, 1), :]], axis=1
            )
            best = jnp.max(score, axis=0, keepdims=True) + bias
            top = best if top is None else jnp.maximum(top, best)
            scores.append(score)
            shifts.append(bias)
        weights = [jnp.exp(scores[s] - (top - shifts[s])) for s in range(section_count)]
        total = sum(jnp.sum(weight, axis=0, keepdims=True) for weight in weights)
        inverse = 1.0 / total
        probs = [weight * inverse for weight in weights]
        probs_low = jnp.concatenate([prob.astype(BF16) for prob in probs], axis=0)
        out_stack = contract(probs_low, value_rows, 0, 0)
        pulls = [probs[s] * dprob[s * BLK : (s + 1) * BLK] for s in range(section_count)]
        delta = sum(jnp.sum(pull, axis=0, keepdims=True) for pull in pulls)
        dscores = [pulls[s] - probs[s] * delta for s in range(section_count)]
        dscore_low = jnp.concatenate([dscore.astype(BF16) for dscore in dscores], axis=0)
        value_terms = contract(probs_low, grad_stack, 1, 0)
        key_terms = contract(dscore_low, q_stack, 1, 0)
        dq_stack = contract(dscore_low, key_rows, 0, 0)
        out_ref[:, mine] = jnp.where(low, out_stack[:BLK], out_stack[BLK:]).astype(BF16)
        dq_ref[:, mine] = (jnp.where(low, dq_stack[:BLK], dq_stack[BLK:]) * 0.125).astype(BF16)
        pay = pay_ref[0]
        for s in range(section_count):
            sums = jnp.sum(dscores[s], axis=0, keepdims=True)
            even = jnp.sum(sums[:, :BLK], axis=1, keepdims=True)
            odd = jnp.sum(sums[:, BLK:], axis=1, keepdims=True)
            pay = jnp.where(lanes == s * H + head, even, pay)
            pay = jnp.where(lanes == s * H + head + 1, odd, pay)
            key_term = key_terms[s * BLK : (s + 1) * BLK]
            value_term = value_terms[s * BLK : (s + 1) * BLK]
            if s == 0:
                own_ref[0:BLK, here] = key_term
                own_ref[BLK : 2 * BLK, here] = value_term
            else:
                term_refs[s - 1][0:BLK, here] = key_term.astype(BF16)
                term_refs[s - 1][BLK : 2 * BLK, here] = value_term.astype(BF16)
        pay_ref[...] = jnp.broadcast_to(pay[:, None, :], pay_ref.shape)
        return carry

    lax.fori_loop(0, half_features // PAIR_LANES, one_pair, 0, unroll=UNROLL)


def attention_half(half, copies, scalars, table_rows, rows, near, far, previous):
    near_count, far_count = len(near), len(far)
    section_count = 1 + near_count + far_count
    row_count, feature_count = rows[0].shape
    half_features = feature_count // HALVES
    half_heads = half_features // DH
    vmem = pl.BlockSpec(memory_space=pltpu.VMEM)
    operands = [*scalars, table_rows, *rows, *near, *far]
    in_specs = [vmem] * len(operands)
    covered = (half + 1) * half_features
    packed = jax.ShapeDtypeStruct((2 * row_count, half_features), BF16)
    out_shape = [
        *[jax.ShapeDtypeStruct((row_count, covered), BF16)] * 2,
        jax.ShapeDtypeStruct((2 * row_count, half_features), F32),
        *[packed] * (section_count - 1),
        jax.ShapeDtypeStruct((1 if previous is None else copies, 1, LANES), F32),
    ]
    if previous is None:
        out_shape += [
            jax.ShapeDtypeStruct((section_count * BLK, BLK), F32),
            jax.ShapeDtypeStruct((section_count, H, LANES), F32),
        ]
    else:
        operands += [*previous[-2:], previous[-3], *previous[:2]]
        in_specs += [vmem] * 5
    return pl.pallas_call(
        functools.partial(attention_body, near_count, far_count, half),
        in_specs=in_specs,
        out_specs=[vmem] * len(out_shape),
        out_shape=out_shape,
        compiler_params=pltpu.CompilerParams(vmem_limit_bytes=VMEM_LIMIT),
        cost_estimate=pl.CostEstimate(
            flops=FLOPS, bytes_accessed=4 * 2**20, transcendentals=section_count * half_heads * BLK * BLK
        ),
        name="attention",
    )(*operands)


def gather_body(*refs):
    total = refs[0][...]
    for ref in refs[1:-1]:
        total = total + ref[...].astype(F32)
    refs[-1][...] = total


def gather_terms(own, terms):
    vmem = pl.BlockSpec(memory_space=pltpu.VMEM)
    return pl.pallas_call(
        gather_body,
        in_specs=[vmem] * (1 + len(terms)),
        out_specs=vmem,
        out_shape=jax.ShapeDtypeStruct(own.shape, F32),
        compiler_params=pltpu.CompilerParams(vmem_limit_bytes=VMEM_LIMIT),
        cost_estimate=pl.CostEstimate(flops=2**19, bytes_accessed=2**21, transcendentals=0),
        name="gather",
    )(own, *terms)


def finish_body(*refs):
    one_ref, two_ref, *term_refs = refs[:-2]
    half_features = one_ref.shape[1]
    for out_ref, block in zip(refs[-2:], (slice(0, BLK), slice(BLK, 2 * BLK))):
        out_ref[:, :half_features] = one_ref[block, :].astype(BF16)
        total = two_ref[block, :]
        for ref in term_refs:
            total = total + ref[block, :].astype(F32)
        out_ref[:, half_features:] = total.astype(BF16)


def finish(one, two, terms):
    vmem = pl.BlockSpec(memory_space=pltpu.VMEM)
    out = jax.ShapeDtypeStruct((one.shape[0] // 2, HALVES * one.shape[1]), BF16)
    return pl.pallas_call(
        finish_body,
        in_specs=[vmem] * (2 + len(terms)),
        out_specs=[vmem, vmem],
        out_shape=[out, out],
        compiler_params=pltpu.CompilerParams(vmem_limit_bytes=VMEM_LIMIT),
        cost_estimate=pl.CostEstimate(flops=2**19, bytes_accessed=2**21, transcendentals=0),
        name="finish",
    )(one, two, *terms)


def table_part(section_count, gathered):
    count = gathered.shape[0]
    lanes = lane_iota((count, LANES))
    column = jnp.where(lanes < NB, lanes, lanes - NB).astype(F32)
    section = jnp.right_shift(lanes, 4)
    high = gathered.astype(BF16)
    low = (gathered - high.astype(F32)).astype(BF16)
    row_hot = (lane_iota((count, NB)).astype(F32) == gathered[:, BUCKET_LANE : BUCKET_LANE + 1]).astype(BF16)
    spread = jnp.bitwise_and(row_iota((LANES, H * NB)), H - 1) == jnp.right_shift(
        lane_iota((LANES, H * NB)), 6
    )
    spread = jnp.where(spread, 1.0, 0.0).astype(BF16)
    pieces = []
    for s in range(section_count):
        for part in (high, low):
            pieces.append(jnp.where(section == s, part, jnp.zeros_like(part)))
    wide = contract(jnp.concatenate(pieces, axis=0), spread, 1, 0)
    masked = []
    for s in range(section_count):
        hot = column == gathered[:, BUCKET_LANE + s : BUCKET_LANE + s + 1]
        hot = jnp.concatenate([hot.astype(F32)] * (H * NB // LANES), axis=1)
        for part in range(2):
            start = (2 * s + part) * count
            masked.append((wide[start : start + count] * hot).astype(BF16))
    rows = jnp.concatenate([row_hot] * (2 * section_count), axis=0)
    return contract(rows, jnp.concatenate(masked, axis=0), 0, 0)


def table_body(section_count, gathered_ref, table_ref, scratch, total):
    count = gathered_ref.shape[0]

    def copy_row(row, carry):
        scratch[pl.ds(row, 1), :] = gathered_ref[row]
        return carry

    lax.fori_loop(0, count, copy_row, 0, unroll=8)
    if count <= TABLE_ROWS:
        table = table_part(section_count, scratch[...])
    else:
        total[...] = jnp.zeros_like(total)

        def add_part(step, carry):
            start = pl.multiple_of(step * TABLE_ROWS, TABLE_ROWS)
            total[...] += table_part(section_count, scratch[pl.ds(start, TABLE_ROWS), :])
            return carry

        lax.fori_loop(0, count // TABLE_ROWS, add_part, 0)
        table = total[...]
    for head in range(H):
        table_ref[head] = table[:, head * NB : (head + 1) * NB]


def table_of(gathered, section_count):
    vmem = pl.BlockSpec(memory_space=pltpu.VMEM)
    return pl.pallas_call(
        functools.partial(table_body, section_count),
        in_specs=[vmem],
        out_specs=vmem,
        out_shape=jax.ShapeDtypeStruct((H, NB, NB), F32),
        scratch_shapes=[
            pltpu.VMEM((gathered.shape[0], LANES), F32),
            pltpu.VMEM((NB, H * NB), F32),
        ],
        compiler_params=pltpu.CompilerParams(vmem_limit_bytes=VMEM_LIMIT),
        name="table",
    )(gathered)


def in_hbm(array):
    return pltpu.with_memory_space_constraint(array, pltpu.HBM)


def pack_body(*refs):
    mask_hbm, bucket_hbm, seg_hbm, key_hbm, value_hbm = refs[:5]
    first_ref, seg_ref, param_ref, mask_ref, bucket_ref, sems = refs[5:]
    half_features = first_ref.shape[1]
    small = [(mask_hbm, mask_ref), (bucket_hbm, bucket_ref), (seg_hbm, seg_ref)]
    copies = [
        pltpu.make_async_copy(source, target, sems.at[i]) for i, (source, target) in enumerate(small)
    ]
    for row, source in ((0, key_hbm), (BLK, value_hbm)):
        copies.append(
            pltpu.make_async_copy(
                source.at[:, pl.ds(0, half_features)],
                first_ref.at[pl.ds(row, BLK), :],
                sems.at[len(copies)],
            )
        )
    for copy in copies:
        copy.start()
    for copy in copies[: len(small)]:
        copy.wait()
    top = row_iota((INFO, LANES)) == 0
    bucket = jnp.broadcast_to(bucket_ref[...], (INFO, LANES))
    info = jnp.where(top, seg_ref[...], bucket).astype(F32).astype(BF16)
    for start in range(0, half_features, LANES):
        first_ref[2 * BLK : 2 * BLK + INFO, start : start + LANES] = info
    lines = row_iota((2 * INFO, LANES))
    params = jnp.where(lines == INFO, bucket_ref[...].astype(F32), 0.0)
    for s in range(1, mask_ref.shape[1]):
        shut = jnp.where(mask_ref[:, s : s + 1] != 0, 0.0, MASKED)
        params = jnp.where(lines == s, shut, params)
    param_ref[...] = params
    for copy in copies[len(small) :]:
        copy.wait()


def pack(mask, bucket, seg, keys, values):
    row_count, feature_count = keys.shape
    vmem = pl.BlockSpec(memory_space=pltpu.VMEM)
    hbm = pl.BlockSpec(memory_space=pltpu.HBM)
    return pl.pallas_call(
        pack_body,
        in_specs=[hbm, pl.BlockSpec(memory_space=pl.ANY), hbm, hbm, hbm],
        out_specs=[vmem] * 3,
        out_shape=[
            jax.ShapeDtypeStruct((2 * row_count + INFO, feature_count // HALVES), BF16),
            jax.ShapeDtypeStruct(seg.shape, jnp.int32),
            jax.ShapeDtypeStruct((2 * INFO, LANES), F32),
        ],
        scratch_shapes=[
            pltpu.VMEM(mask.shape, jnp.int32),
            pltpu.VMEM(bucket.shape, jnp.int32),
            pltpu.SemaphoreType.DMA((5,)),
        ],
        compiler_params=pltpu.CompilerParams(vmem_limit_bytes=VMEM_LIMIT),
        name="pack",
    )(*[bucket if a is bucket else in_hbm(a) for a in (mask, bucket, seg, keys, values)])


def load_body(first_ref, *refs):
    sources, targets, sems = refs[:5], refs[5:10], refs[10]
    whole_ref, second_ref = targets[:2]
    half_features = first_ref.shape[1]
    copies = []

    def add(source, target):
        copies.append(pltpu.make_async_copy(source, target, sems.at[len(copies)]))
        copies[-1].start()

    for row, source in ((0, sources[0]), (BLK, sources[1])):
        add(source, whole_ref.at[pl.ds(row, BLK), :])
        add(source.at[:, pl.ds(half_features, half_features)], second_ref.at[pl.ds(row, BLK), :])
    for source, target in zip(sources[2:], targets[2:]):
        add(source, target)
    info = first_ref[2 * BLK : 2 * BLK + INFO, :]
    for half in range(HALVES):
        window = slice(half * half_features, (half + 1) * half_features)
        whole_ref[2 * BLK : 2 * BLK + INFO, window] = info
    for copy in copies:
        copy.wait()


def load(first, keys, values, *arrays):
    row_count, feature_count = keys.shape
    vmem = pl.BlockSpec(memory_space=pltpu.VMEM)
    out_shape = [
        jax.ShapeDtypeStruct((2 * row_count + INFO, feature_count), BF16),
        jax.ShapeDtypeStruct((2 * row_count, feature_count // HALVES), BF16),
        *[jax.ShapeDtypeStruct(a.shape, a.dtype) for a in arrays],
    ]
    return pl.pallas_call(
        load_body,
        in_specs=[vmem] + [pl.BlockSpec(memory_space=pltpu.HBM)] * 5,
        out_specs=[vmem] * 5,
        out_shape=out_shape,
        scratch_shapes=[pltpu.SemaphoreType.DMA((4 + len(arrays),))],
        compiler_params=pltpu.CompilerParams(vmem_limit_bytes=VMEM_LIMIT),
        name="load",
    )(first, *[in_hbm(a) for a in (keys, values, *arrays)])


def after(value, *earlier):
    return lax.optimization_barrier((value, *earlier))[0]


def double(block, axis, mask):
    return jnp.concatenate([block, from_partner(block, axis, mask)], axis=0)


def local(queries, keys, values, d_out, segment_ids, block_bucket, block_mask, bias_table):
    level_count = lax.axis_size("seq").bit_length() - 1
    far_levels = list(range(level_count))
    last = far_levels[-2:]

    def send(value, level):
        return from_partner(value, "seq", 1 << level)

    first, *scalars = pack(
        block_mask.reshape(1, -1), block_bucket, segment_ids, keys[0], values[0]
    )
    whole, second, query_rows, grad_rows, table_rows = load(
        first, keys[0], values[0], queries[0], d_out[0], bias_table.reshape(H * NB, NB)
    )
    rows = [query_rows, grad_rows, whole]
    far = [{}, {}]
    for level in reversed(far_levels):
        far[0][level] = send(first, level)
    for level in far_levels:
        gate = (far[0][0], query_rows) if level else (far[0][last[-1]], query_rows)
        far[1][level] = send(after(second, *gate), level)
    near_list = []
    near_count = len(near_list)

    device_count = lax.axis_size("dp") * lax.axis_size("seq")
    one = attention_half(
        0, device_count, scalars, table_rows, rows, near_list, [far[0][level] for level in far_levels], None
    )
    middle = [level for level in range(level_count) if level not in last]
    terms = one[3 : 3 + level_count]
    back_one = {level: send(terms[level], level) for level in [*last, *middle[1:]]}
    late = [back_one[level] for level in last]
    two = attention_half(
        1, device_count, scalars, table_rows, rows, near_list, [far[1][level] for level in far_levels], one
    )
    terms = two[3 : 3 + level_count]
    back_two = {level: send(terms[level], level) for level in last}
    block = two[3 + level_count]
    gathered = lax.all_to_all(block, ("dp", "seq"), 0, 0, tiled=True)
    for level in middle:
        back_two[level] = send(after(terms[level], *late, *[back_one[m] for m in middle[1:]]), level)
    back_one[0] = send(after(one[3], *late), 0)
    sum_one = gather_terms(one[2], list(back_one.values()))
    sum_two = gather_terms(two[2], [back_two[level] for level in last])
    d_keys, d_values = finish(sum_one, sum_two, [back_two[level] for level in middle])
    table_total = table_of(after(gathered, d_keys), level_count + 1)
    return (two[0][None], two[1][None], d_keys[None], d_values[None], table_total)


def solution(mesh):
    rows = P("dp", "seq", None)
    in_specs = (
        rows,
        rows,
        rows,
        rows,
        P("dp", "seq"),
        P("dp", "seq"),
        P("dp", "seq", None, None),
        P(),
    )
    return jax.shard_map(
        local, mesh=mesh, in_specs=in_specs, out_specs=(rows,) * 4 + (P(),), check_vma=False
    )
```

```python
import functools

import jax
import jax.numpy as jnp
from jax import lax
from jax.experimental import pallas as pl
from jax.experimental.pallas import tpu as pltpu
from jax.sharding import PartitionSpec as P

H = 16
DH = 64
NB = 64
BLK = 128
HALVES = 2
INFO = 8
LANES = 128
PAIR_LANES = 2 * DH
BUCKET_LANE = 112
MASKED = -1e30
TABLE_ROWS = 32
UNROLL = 4
VMEM_LIMIT = 16 * 2**20
FLOPS = 2 * 10**10

F32 = jnp.float32
BF16 = jnp.bfloat16


def contract(a, b, dim_a, dim_b):
    return lax.dot_general(a, b, (((dim_a,), (dim_b,)), ((), ())), preferred_element_type=F32)


def from_partner(value, axis, mask):
    pairs = [(source, source ^ mask) for source in range(lax.axis_size(axis))]
    return lax.ppermute(value, axis, pairs)


def lane_iota(shape):
    return lax.broadcasted_iota(jnp.int32, shape, len(shape) - 1)


def row_iota(shape):
    return lax.broadcasted_iota(jnp.int32, shape, len(shape) - 2)


def split_pair(pair, low):
    zero = jnp.zeros_like(pair)
    return jnp.concatenate([jnp.where(low, pair, zero), jnp.where(low, zero, pair)], axis=0)


def attention_body(near_count, far_count, half, *refs):
    section_count = 1 + near_count + far_count
    first = half == 0
    refs = list(refs)

    def take(count):
        taken, refs[:] = refs[:count], refs[count:]
        return taken

    seg_ref, param_ref, table_ref, q_ref, do_ref, own_pack_ref = take(6)
    near_refs = take(near_count)
    far_refs = take(far_count)
    if not first:
        masks, biases, pay_in_ref = take(3)
        earlier = take(2)
    out_ref, dq_ref = take(2)
    own_ref, *term_refs, pay_ref = take(1 + section_count)
    if first:
        masks, biases = take(2)
    half_features = own_ref.shape[1]
    half_heads = half_features // DH
    info_row = half_features // PAIR_LANES * 2 * BLK

    if first:
        own_bucket = param_ref[INFO : INFO + 1, :]
        seg_rows = seg_ref[...].astype(F32)
        in_row = row_iota((H, NB, LANES)).astype(F32) == own_bucket
        pay = jnp.zeros((1, LANES), F32)
        for s in range(section_count):
            if s == 0:
                seg_cols = seg_rows
                bucket = own_bucket
            else:
                info = far_refs[s - 1][info_row : info_row + INFO, :].astype(F32)
                seg_cols = info[0:1]
                bucket = info[1:2]
            cols = jnp.broadcast_to(seg_cols, (BLK, BLK)).T
            masks[s * BLK : (s + 1) * BLK, :] = jnp.where(
                cols == seg_rows, jnp.broadcast_to(param_ref[s : s + 1, :], (BLK, BLK)), MASKED
            )
            hot = (row_iota((NB, LANES)).astype(F32) == bucket).astype(BF16)
            picked = contract(table_ref[...], hot, 1, 0).reshape(H, NB, LANES)
            biases[s] = jnp.sum(jnp.where(in_row, picked, 0.0), axis=1)
            pay = jnp.where(lane_iota(pay.shape) == BUCKET_LANE + s, bucket, pay)
        pay_ref[0] = pay
    else:
        pay_ref[0] = pay_in_ref[0]
        for source, target in zip(earlier, [out_ref, dq_ref]):
            target[:, 0 : half * half_features] = source[...]

    low = lane_iota((BLK, PAIR_LANES)) < DH
    lanes = lane_iota((1, LANES))

    def one_pair(pair, carry):
        here = pl.ds(pl.multiple_of(pair * PAIR_LANES, PAIR_LANES), PAIR_LANES)
        there = pl.ds(
            pl.multiple_of(half * half_features + pair * PAIR_LANES, PAIR_LANES), PAIR_LANES
        )
        mine = here if first else there
        key_block = pl.ds(pl.multiple_of(pair * 2 * BLK, BLK), BLK)
        value_block = pl.ds(pl.multiple_of(pair * 2 * BLK + BLK, BLK), BLK)
        head = half * half_heads + 2 * pair
        q_stack = split_pair(q_ref[:, there] * jnp.asarray(0.125, BF16), low)
        grad_stack = split_pair(do_ref[:, there], low)
        key_rows = jnp.concatenate(
            [own_pack_ref[0:BLK, there]]
            + [r[key_block, :] for r in far_refs],
            axis=0,
        )
        value_rows = jnp.concatenate(
            [own_pack_ref[BLK : 2 * BLK, there]]
            + [r[value_block, :] for r in far_refs],
            axis=0,
        )
        raw = contract(key_rows, q_stack, 1, 1)
        dprob = contract(value_rows, grad_stack, 1, 1)
        scores = []
        shifts = []
        top = None
        for s in range(section_count):
            block = slice(s * BLK, (s + 1) * BLK)
            mask = masks[block, :]
            score = raw[block] + jnp.concatenate([mask, mask], axis=1)
            bias = jnp.concatenate(
                [biases[s, pl.ds(head, 1), :], biases[s, pl.ds(head + 1, 1), :]], axis=1
            )
            best = jnp.max(score, axis=0, keepdims=True) + bias
            top = best if top is None else jnp.maximum(top, best)
            scores.append(score)
            shifts.append(bias)
        weights = [jnp.exp(scores[s] - (top - shifts[s])) for s in range(section_count)]
        total = sum(jnp.sum(weight, axis=0, keepdims=True) for weight in weights)
        inverse = 1.0 / total
        probs = [weight * inverse for weight in weights]
        probs_low = jnp.concatenate([prob.astype(BF16) for prob in probs], axis=0)
        out_stack = contract(probs_low, value_rows, 0, 0)
        pulls = [probs[s] * dprob[s * BLK : (s + 1) * BLK] for s in range(section_count)]
        delta = sum(jnp.sum(pull, axis=0, keepdims=True) for pull in pulls)
        dscores = [pulls[s] - probs[s] * delta for s in range(section_count)]
        dscore_low = jnp.concatenate([dscore.astype(BF16) for dscore in dscores], axis=0)
        value_terms = contract(probs_low, grad_stack, 1, 0)
        key_terms = contract(dscore_low, q_stack, 1, 0)
        dq_stack = contract(dscore_low, key_rows, 0, 0)
        out_ref[:, mine] = jnp.where(low, out_stack[:BLK], out_stack[BLK:]).astype(BF16)
        dq_ref[:, mine] = (jnp.where(low, dq_stack[:BLK], dq_stack[BLK:]) * 0.125).astype(BF16)
        pay = pay_ref[0]
        for s in range(section_count):
            sums = jnp.sum(dscores[s], axis=0, keepdims=True)
            even = jnp.sum(sums[:, :BLK], axis=1, keepdims=True)
            odd = jnp.sum(sums[:, BLK:], axis=1, keepdims=True)
            pay = jnp.where(lanes == s * H + head, even, pay)
            pay = jnp.where(lanes == s * H + head + 1, odd, pay)
            key_term = key_terms[s * BLK : (s + 1) * BLK]
            value_term = value_terms[s * BLK : (s + 1) * BLK]
            if s == 0:
                own_ref[0:BLK, here] = key_term
                own_ref[BLK : 2 * BLK, here] = value_term
            else:
                term_refs[s - 1][0:BLK, here] = key_term.astype(BF16)
                term_refs[s - 1][BLK : 2 * BLK, here] = value_term.astype(BF16)
        pay_ref[...] = jnp.broadcast_to(pay[:, None, :], pay_ref.shape)
        return carry

    lax.fori_loop(0, half_features // PAIR_LANES, one_pair, 0, unroll=UNROLL)


def attention_half(half, copies, scalars, table_rows, rows, near, far, previous):
    near_count, far_count = len(near), len(far)
    section_count = 1 + near_count + far_count
    row_count, feature_count = rows[0].shape
    half_features = feature_count // HALVES
    half_heads = half_features // DH
    vmem = pl.BlockSpec(memory_space=pltpu.VMEM)
    operands = [*scalars, table_rows, *rows, *near, *far]
    in_specs = [vmem] * len(operands)
    covered = (half + 1) * half_features
    packed = jax.ShapeDtypeStruct((2 * row_count, half_features), BF16)
    out_shape = [
        *[jax.ShapeDtypeStruct((row_count, covered), BF16)] * 2,
        jax.ShapeDtypeStruct((2 * row_count, half_features), F32),
        *[packed] * (section_count - 1),
        jax.ShapeDtypeStruct((1 if previous is None else copies, 1, LANES), F32),
    ]
    if previous is None:
        out_shape += [
            jax.ShapeDtypeStruct((section_count * BLK, BLK), F32),
            jax.ShapeDtypeStruct((section_count, H, LANES), F32),
        ]
    else:
        operands += [*previous[-2:], previous[-3], *previous[:2]]
        in_specs += [vmem] * 5
    return pl.pallas_call(
        functools.partial(attention_body, near_count, far_count, half),
        in_specs=in_specs,
        out_specs=[vmem] * len(out_shape),
        out_shape=out_shape,
        compiler_params=pltpu.CompilerParams(vmem_limit_bytes=VMEM_LIMIT),
        cost_estimate=pl.CostEstimate(
            flops=FLOPS, bytes_accessed=4 * 2**20, transcendentals=section_count * half_heads * BLK * BLK
        ),
        name="attention",
    )(*operands)


def gather_body(*refs):
    total = refs[0][...]
    for ref in refs[1:-1]:
        total = total + ref[...].astype(F32)
    refs[-1][...] = total


def gather_terms(own, terms):
    vmem = pl.BlockSpec(memory_space=pltpu.VMEM)
    return pl.pallas_call(
        gather_body,
        in_specs=[vmem] * (1 + len(terms)),
        out_specs=vmem,
        out_shape=jax.ShapeDtypeStruct(own.shape, F32),
        compiler_params=pltpu.CompilerParams(vmem_limit_bytes=VMEM_LIMIT),
        cost_estimate=pl.CostEstimate(flops=2**19, bytes_accessed=2**21, transcendentals=0),
        name="gather",
    )(own, *terms)


def finish_body(*refs):
    one_ref, two_ref, *term_refs = refs[:-2]
    half_features = one_ref.shape[1]
    for out_ref, block in zip(refs[-2:], (slice(0, BLK), slice(BLK, 2 * BLK))):
        out_ref[:, :half_features] = one_ref[block, :].astype(BF16)
        total = two_ref[block, :]
        for ref in term_refs:
            total = total + ref[block, :].astype(F32)
        out_ref[:, half_features:] = total.astype(BF16)


def finish(one, two, terms):
    vmem = pl.BlockSpec(memory_space=pltpu.VMEM)
    out = jax.ShapeDtypeStruct((one.shape[0] // 2, HALVES * one.shape[1]), BF16)
    return pl.pallas_call(
        finish_body,
        in_specs=[vmem] * (2 + len(terms)),
        out_specs=[vmem, vmem],
        out_shape=[out, out],
        compiler_params=pltpu.CompilerParams(vmem_limit_bytes=VMEM_LIMIT),
        cost_estimate=pl.CostEstimate(flops=2**19, bytes_accessed=2**21, transcendentals=0),
        name="finish",
    )(one, two, *terms)


def table_part(section_count, gathered):
    count = gathered.shape[0]
    lanes = lane_iota((count, LANES))
    column = jnp.where(lanes < NB, lanes, lanes - NB).astype(F32)
    section = jnp.right_shift(lanes, 4)
    high = gathered.astype(BF16)
    low = (gathered - high.astype(F32)).astype(BF16)
    row_hot = (lane_iota((count, NB)).astype(F32) == gathered[:, BUCKET_LANE : BUCKET_LANE + 1]).astype(BF16)
    spread = jnp.bitwise_and(row_iota((LANES, H * NB)), H - 1) == jnp.right_shift(
        lane_iota((LANES, H * NB)), 6
    )
    spread = jnp.where(spread, 1.0, 0.0).astype(BF16)
    pieces = []
    for s in range(section_count):
        for part in (high, low):
            pieces.append(jnp.where(section == s, part, jnp.zeros_like(part)))
    wide = contract(jnp.concatenate(pieces, axis=0), spread, 1, 0)
    masked = []
    for s in range(section_count):
        hot = column == gathered[:, BUCKET_LANE + s : BUCKET_LANE + s + 1]
        hot = jnp.concatenate([hot.astype(F32)] * (H * NB // LANES), axis=1)
        for part in range(2):
            start = (2 * s + part) * count
            masked.append((wide[start : start + count] * hot).astype(BF16))
    rows = jnp.concatenate([row_hot] * (2 * section_count), axis=0)
    return contract(rows, jnp.concatenate(masked, axis=0), 0, 0)


def table_body(section_count, gathered_ref, table_ref, scratch, total):
    count = gathered_ref.shape[0]

    def copy_row(row, carry):
        scratch[pl.ds(row, 1), :] = gathered_ref[row]
        return carry

    lax.fori_loop(0, count, copy_row, 0, unroll=8)
    if count <= TABLE_ROWS:
        table = table_part(section_count, scratch[...])
    else:
        total[...] = jnp.zeros_like(total)

        def add_part(step, carry):
            start = pl.multiple_of(step * TABLE_ROWS, TABLE_ROWS)
            total[...] += table_part(section_count, scratch[pl.ds(start, TABLE_ROWS), :])
            return carry

        lax.fori_loop(0, count // TABLE_ROWS, add_part, 0)
        table = total[...]
    for head in range(H):
        table_ref[head] = table[:, head * NB : (head + 1) * NB]


def table_of(gathered, section_count):
    vmem = pl.BlockSpec(memory_space=pltpu.VMEM)
    return pl.pallas_call(
        functools.partial(table_body, section_count),
        in_specs=[vmem],
        out_specs=vmem,
        out_shape=jax.ShapeDtypeStruct((H, NB, NB), F32),
        scratch_shapes=[
            pltpu.VMEM((gathered.shape[0], LANES), F32),
            pltpu.VMEM((NB, H * NB), F32),
        ],
        compiler_params=pltpu.CompilerParams(vmem_limit_bytes=VMEM_LIMIT),
        name="table",
    )(gathered)


def in_hbm(array):
    return pltpu.with_memory_space_constraint(array, pltpu.HBM)


def pack_body(*refs):
    mask_hbm, bucket_hbm, seg_hbm, key_hbm, value_hbm = refs[:5]
    first_ref, seg_ref, param_ref, mask_ref, bucket_ref, sems = refs[5:]
    pairs = (first_ref.shape[0] - INFO) // (2 * BLK)
    small = [(mask_hbm, mask_ref), (bucket_hbm, bucket_ref), (seg_hbm, seg_ref)]
    copies = [
        pltpu.make_async_copy(source, target, sems.at[i]) for i, (source, target) in enumerate(small)
    ]
    for pair in range(pairs):
        for row, source in ((0, key_hbm), (BLK, value_hbm)):
            copies.append(
                pltpu.make_async_copy(
                    source.at[:, pl.ds(pair * PAIR_LANES, PAIR_LANES)],
                    first_ref.at[pl.ds(pair * 2 * BLK + row, BLK), :],
                    sems.at[len(copies)],
                )
            )
    for copy in copies:
        copy.start()
    for copy in copies[: len(small)]:
        copy.wait()
    top = row_iota((INFO, LANES)) == 0
    bucket = jnp.broadcast_to(bucket_ref[...], (INFO, LANES))
    info = jnp.where(top, seg_ref[...], bucket).astype(F32).astype(BF16)
    first_ref[pairs * 2 * BLK : pairs * 2 * BLK + INFO, :] = info
    lines = row_iota((2 * INFO, LANES))
    params = jnp.where(lines == INFO, bucket_ref[...].astype(F32), 0.0)
    for s in range(1, mask_ref.shape[1]):
        shut = jnp.where(mask_ref[:, s : s + 1] != 0, 0.0, MASKED)
        params = jnp.where(lines == s, shut, params)
    param_ref[...] = params
    for copy in copies[len(small) :]:
        copy.wait()


def pack(mask, bucket, seg, keys, values):
    pairs = keys.shape[1] // HALVES // PAIR_LANES
    vmem = pl.BlockSpec(memory_space=pltpu.VMEM)
    hbm = pl.BlockSpec(memory_space=pltpu.HBM)
    return pl.pallas_call(
        pack_body,
        in_specs=[hbm, pl.BlockSpec(memory_space=pl.ANY), hbm, hbm, hbm],
        out_specs=[vmem] * 3,
        out_shape=[
            jax.ShapeDtypeStruct((pairs * 2 * BLK + INFO, PAIR_LANES), BF16),
            jax.ShapeDtypeStruct(seg.shape, jnp.int32),
            jax.ShapeDtypeStruct((2 * INFO, LANES), F32),
        ],
        scratch_shapes=[
            pltpu.VMEM(mask.shape, jnp.int32),
            pltpu.VMEM(bucket.shape, jnp.int32),
            pltpu.SemaphoreType.DMA((3 + 2 * pairs,)),
        ],
        compiler_params=pltpu.CompilerParams(vmem_limit_bytes=VMEM_LIMIT),
        name="pack",
    )(*[bucket if a is bucket else in_hbm(a) for a in (mask, bucket, seg, keys, values)])


def load_body(first_ref, *refs):
    sources, targets, sems = refs[:5], refs[5:10], refs[10]
    whole_ref, second_ref = targets[:2]
    pairs = second_ref.shape[0] // (2 * BLK)
    copies = []

    def add(source, target):
        copies.append(pltpu.make_async_copy(source, target, sems.at[len(copies)]))
        copies[-1].start()

    for row, source in ((0, sources[0]), (BLK, sources[1])):
        for pair in range(pairs):
            window = pl.ds((pairs + pair) * PAIR_LANES, PAIR_LANES)
            add(source.at[:, window], second_ref.at[pl.ds(pair * 2 * BLK + row, BLK), :])
        add(source, whole_ref.at[pl.ds(row, BLK), :])
    for source, target in zip(sources[2:], targets[2:]):
        add(source, target)
    for copy in copies:
        copy.wait()


def load(first, keys, values, *arrays):
    row_count, feature_count = keys.shape
    pairs = feature_count // HALVES // PAIR_LANES
    vmem = pl.BlockSpec(memory_space=pltpu.VMEM)
    out_shape = [
        jax.ShapeDtypeStruct((2 * row_count, feature_count), BF16),
        jax.ShapeDtypeStruct((pairs * 2 * BLK, PAIR_LANES), BF16),
        *[jax.ShapeDtypeStruct(a.shape, a.dtype) for a in arrays],
    ]
    return pl.pallas_call(
        load_body,
        in_specs=[vmem] + [pl.BlockSpec(memory_space=pltpu.HBM)] * 5,
        out_specs=[vmem] * 5,
        out_shape=out_shape,
        scratch_shapes=[pltpu.SemaphoreType.DMA((2 + 2 * pairs + len(arrays),))],
        compiler_params=pltpu.CompilerParams(vmem_limit_bytes=VMEM_LIMIT),
        name="load",
    )(first, *[in_hbm(a) for a in (keys, values, *arrays)])


def after(value, *earlier):
    return lax.optimization_barrier((value, *earlier))[0]


def double(block, axis, mask):
    return jnp.concatenate([block, from_partner(block, axis, mask)], axis=0)


def local(queries, keys, values, d_out, segment_ids, block_bucket, block_mask, bias_table):
    level_count = lax.axis_size("seq").bit_length() - 1
    far_levels = list(range(level_count))
    last = far_levels[-2:]

    def send(value, level):
        return from_partner(value, "seq", 1 << level)

    first, *scalars = pack(
        block_mask.reshape(1, -1), block_bucket, segment_ids, keys[0], values[0]
    )
    whole, second, query_rows, grad_rows, table_rows = load(
        first, keys[0], values[0], queries[0], d_out[0], bias_table.reshape(H * NB, NB)
    )
    rows = [query_rows, grad_rows, whole]
    far = [{}, {}]
    for level in reversed(far_levels):
        far[0][level] = send(first, level)
    for level in far_levels:
        gate = (far[0][0], query_rows) if level else (far[0][last[-1]], query_rows)
        far[1][level] = send(after(second, *gate), level)
    near_list = []
    near_count = len(near_list)

    device_count = lax.axis_size("dp") * lax.axis_size("seq")
    one = attention_half(
        0, device_count, scalars, table_rows, rows, near_list, [far[0][level] for level in far_levels], None
    )
    middle = [level for level in range(level_count) if level not in last]
    terms = one[3 : 3 + level_count]
    back_one = {level: send(terms[level], level) for level in [*last, *middle[1:]]}
    late = [back_one[level] for level in last]
    two = attention_half(
        1, device_count, scalars, table_rows, rows, near_list, [far[1][level] for level in far_levels], one
    )
    terms = two[3 : 3 + level_count]
    back_two = {level: send(terms[level], level) for level in last}
    block = two[3 + level_count]
    gathered = lax.all_to_all(block, ("dp", "seq"), 0, 0, tiled=True)
    for level in middle:
        back_two[level] = send(after(terms[level], *late, *[back_one[m] for m in middle[1:]]), level)
    back_one[0] = send(after(one[3], *late), 0)
    sum_one = gather_terms(one[2], list(back_one.values()))
    sum_two = gather_terms(two[2], [back_two[level] for level in last])
    d_keys, d_values = finish(sum_one, sum_two, [back_two[level] for level in middle])
    table_total = table_of(after(gathered, d_keys), level_count + 1)
    return (two[0][None], two[1][None], d_keys[None], d_values[None], table_total)


def solution(mesh):
    rows = P("dp", "seq", None)
    in_specs = (
        rows,
        rows,
        rows,
        rows,
        P("dp", "seq"),
        P("dp", "seq"),
        P("dp", "seq", None, None),
        P(),
    )
    return jax.shard_map(
        local, mesh=mesh, in_specs=in_specs, out_specs=(rows,) * 4 + (P(),), check_vma=False
    )
```

```python
import functools

import jax
import jax.numpy as jnp
from jax import lax
from jax.experimental import pallas as pl
from jax.experimental.pallas import tpu as pltpu
from jax.sharding import PartitionSpec as P

H = 16
DH = 64
NB = 64
BLK = 128
HALVES = 2
INFO = 8
LANES = 128
PAIR_LANES = 2 * DH
BUCKET_LANE = 112
MASKED = -1e30
TABLE_ROWS = 32
TABLE_HEADS = 4
UNROLL = 4
VMEM_LIMIT = 16 * 2**20
FLOPS = 2 * 10**10

F32 = jnp.float32
BF16 = jnp.bfloat16


def contract(a, b, dim_a, dim_b):
    return lax.dot_general(a, b, (((dim_a,), (dim_b,)), ((), ())), preferred_element_type=F32)


def from_partner(value, axis, mask):
    pairs = [(source, source ^ mask) for source in range(lax.axis_size(axis))]
    return lax.ppermute(value, axis, pairs)


def lane_iota(shape):
    return lax.broadcasted_iota(jnp.int32, shape, len(shape) - 1)


def row_iota(shape):
    return lax.broadcasted_iota(jnp.int32, shape, len(shape) - 2)


def split_pair(pair, low):
    zero = jnp.zeros_like(pair)
    return jnp.concatenate([jnp.where(low, pair, zero), jnp.where(low, zero, pair)], axis=0)


def attention_body(near_count, far_count, half, *refs):
    section_count = 1 + near_count + far_count
    first = half == 0
    refs = list(refs)

    def take(count):
        taken, refs[:] = refs[:count], refs[count:]
        return taken

    seg_ref, param_ref, table_ref, q_ref, do_ref, own_pack_ref = take(6)
    near_refs = take(near_count)
    far_refs = take(far_count)
    if not first:
        masks, biases, pay_in_ref = take(3)
        earlier = take(2)
    out_ref, dq_ref = take(2)
    own_ref, *term_refs, pay_ref = take(1 + section_count)
    if first:
        masks, biases = take(2)
    half_features = own_ref.shape[1]
    half_heads = half_features // DH
    info_row = half_features // PAIR_LANES * 2 * BLK

    if first:
        own_bucket = param_ref[INFO : INFO + 1, :]
        seg_rows = seg_ref[...].astype(F32)
        in_row = row_iota((H, NB, LANES)).astype(F32) == own_bucket
        pay = jnp.zeros((1, LANES), F32)
        for s in range(section_count):
            if s == 0:
                seg_cols = seg_rows
                bucket = own_bucket
            else:
                info = far_refs[s - 1][info_row : info_row + INFO, :].astype(F32)
                seg_cols = info[0:1]
                bucket = info[1:2]
            cols = jnp.broadcast_to(seg_cols, (BLK, BLK)).T
            masks[s * BLK : (s + 1) * BLK, :] = jnp.where(
                cols == seg_rows, jnp.broadcast_to(param_ref[s : s + 1, :], (BLK, BLK)), MASKED
            )
            hot = (row_iota((NB, LANES)).astype(F32) == bucket).astype(BF16)
            picked = contract(table_ref[...], hot, 1, 0).reshape(H, NB, LANES)
            biases[s] = jnp.sum(jnp.where(in_row, picked, 0.0), axis=1)
            pay = jnp.where(lane_iota(pay.shape) == BUCKET_LANE + s, bucket, pay)
        pay_ref[0] = pay
    else:
        pay_ref[0] = pay_in_ref[0]
        for source, target in zip(earlier, [out_ref, dq_ref]):
            target[:, 0 : half * half_features] = source[...]

    low = lane_iota((BLK, PAIR_LANES)) < DH
    lanes = lane_iota((1, LANES))

    def one_pair(pair, carry):
        here = pl.ds(pl.multiple_of(pair * PAIR_LANES, PAIR_LANES), PAIR_LANES)
        there = pl.ds(
            pl.multiple_of(half * half_features + pair * PAIR_LANES, PAIR_LANES), PAIR_LANES
        )
        mine = here if first else there
        key_block = pl.ds(pl.multiple_of(pair * 2 * BLK, BLK), BLK)
        value_block = pl.ds(pl.multiple_of(pair * 2 * BLK + BLK, BLK), BLK)
        head = half * half_heads + 2 * pair
        q_stack = split_pair(q_ref[:, there] * jnp.asarray(0.125, BF16), low)
        grad_stack = split_pair(do_ref[:, there], low)
        key_rows = jnp.concatenate(
            [own_pack_ref[0:BLK, there]]
            + [r[key_block, :] for r in far_refs],
            axis=0,
        )
        value_rows = jnp.concatenate(
            [own_pack_ref[BLK : 2 * BLK, there]]
            + [r[value_block, :] for r in far_refs],
            axis=0,
        )
        raw = contract(key_rows, q_stack, 1, 1)
        dprob = contract(value_rows, grad_stack, 1, 1)
        scores = []
        shifts = []
        top = None
        for s in range(section_count):
            block = slice(s * BLK, (s + 1) * BLK)
            mask = masks[block, :]
            score = raw[block] + jnp.concatenate([mask, mask], axis=1)
            bias = jnp.concatenate(
                [biases[s, pl.ds(head, 1), :], biases[s, pl.ds(head + 1, 1), :]], axis=1
            )
            best = jnp.max(score, axis=0, keepdims=True) + bias
            top = best if top is None else jnp.maximum(top, best)
            scores.append(score)
            shifts.append(bias)
        weights = [jnp.exp(scores[s] - (top - shifts[s])) for s in range(section_count)]
        total = sum(jnp.sum(weight, axis=0, keepdims=True) for weight in weights)
        inverse = 1.0 / total
        probs = [weight * inverse for weight in weights]
        probs_low = jnp.concatenate([prob.astype(BF16) for prob in probs], axis=0)
        out_stack = contract(probs_low, value_rows, 0, 0)
        pulls = [probs[s] * dprob[s * BLK : (s + 1) * BLK] for s in range(section_count)]
        delta = sum(jnp.sum(pull, axis=0, keepdims=True) for pull in pulls)
        dscores = [pulls[s] - probs[s] * delta for s in range(section_count)]
        dscore_low = jnp.concatenate([dscore.astype(BF16) for dscore in dscores], axis=0)
        value_terms = contract(probs_low, grad_stack, 1, 0)
        key_terms = contract(dscore_low, q_stack, 1, 0)
        dq_stack = contract(dscore_low, key_rows, 0, 0)
        out_ref[:, mine] = jnp.where(low, out_stack[:BLK], out_stack[BLK:]).astype(BF16)
        dq_ref[:, mine] = (jnp.where(low, dq_stack[:BLK], dq_stack[BLK:]) * 0.125).astype(BF16)
        pay = pay_ref[0]
        for s in range(section_count):
            sums = jnp.sum(dscores[s], axis=0, keepdims=True)
            even = jnp.sum(sums[:, :BLK], axis=1, keepdims=True)
            odd = jnp.sum(sums[:, BLK:], axis=1, keepdims=True)
            pay = jnp.where(lanes == s * H + head, even, pay)
            pay = jnp.where(lanes == s * H + head + 1, odd, pay)
            key_term = key_terms[s * BLK : (s + 1) * BLK]
            value_term = value_terms[s * BLK : (s + 1) * BLK]
            if s == 0:
                own_ref[0:BLK, here] = key_term
                own_ref[BLK : 2 * BLK, here] = value_term
            else:
                term_refs[s - 1][0:BLK, here] = key_term.astype(BF16)
                term_refs[s - 1][BLK : 2 * BLK, here] = value_term.astype(BF16)
        pay_ref[...] = jnp.broadcast_to(pay[:, None, :], pay_ref.shape)
        return carry

    lax.fori_loop(0, half_features // PAIR_LANES, one_pair, 0, unroll=UNROLL)


def attention_half(half, copies, scalars, table_rows, rows, near, far, previous):
    near_count, far_count = len(near), len(far)
    section_count = 1 + near_count + far_count
    row_count, feature_count = rows[0].shape
    half_features = feature_count // HALVES
    half_heads = half_features // DH
    vmem = pl.BlockSpec(memory_space=pltpu.VMEM)
    operands = [*scalars, table_rows, *rows, *near, *far]
    in_specs = [vmem] * len(operands)
    covered = (half + 1) * half_features
    packed = jax.ShapeDtypeStruct((2 * row_count, half_features), BF16)
    out_shape = [
        *[jax.ShapeDtypeStruct((row_count, covered), BF16)] * 2,
        jax.ShapeDtypeStruct((2 * row_count, half_features), F32),
        *[packed] * (section_count - 1),
        jax.ShapeDtypeStruct((1 if previous is None else copies, 1, LANES), F32),
    ]
    if previous is None:
        out_shape += [
            jax.ShapeDtypeStruct((section_count * BLK, BLK), F32),
            jax.ShapeDtypeStruct((section_count, H, LANES), F32),
        ]
    else:
        operands += [*previous[-2:], previous[-3], *previous[:2]]
        in_specs += [vmem] * 5
    return pl.pallas_call(
        functools.partial(attention_body, near_count, far_count, half),
        in_specs=in_specs,
        out_specs=[vmem] * len(out_shape),
        out_shape=out_shape,
        compiler_params=pltpu.CompilerParams(vmem_limit_bytes=VMEM_LIMIT),
        cost_estimate=pl.CostEstimate(
            flops=FLOPS, bytes_accessed=4 * 2**20, transcendentals=section_count * half_heads * BLK * BLK
        ),
        name="attention",
    )(*operands)


def gather_body(*refs):
    total = refs[0][...]
    for ref in refs[1:-1]:
        total = total + ref[...].astype(F32)
    refs[-1][...] = total


def gather_terms(own, terms):
    vmem = pl.BlockSpec(memory_space=pltpu.VMEM)
    return pl.pallas_call(
        gather_body,
        in_specs=[vmem] * (1 + len(terms)),
        out_specs=vmem,
        out_shape=jax.ShapeDtypeStruct(own.shape, F32),
        compiler_params=pltpu.CompilerParams(vmem_limit_bytes=VMEM_LIMIT),
        cost_estimate=pl.CostEstimate(flops=2**19, bytes_accessed=2**21, transcendentals=0),
        name="gather",
    )(own, *terms)


def finish_body(*refs):
    one_ref, two_ref, *term_refs = refs[:-2]
    half_features = one_ref.shape[1]
    for out_ref, block in zip(refs[-2:], (slice(0, BLK), slice(BLK, 2 * BLK))):
        out_ref[:, :half_features] = one_ref[block, :].astype(BF16)
        total = two_ref[block, :]
        for ref in term_refs:
            total = total + ref[block, :].astype(F32)
        out_ref[:, half_features:] = total.astype(BF16)


def finish(one, two, terms):
    vmem = pl.BlockSpec(memory_space=pltpu.VMEM)
    out = jax.ShapeDtypeStruct((one.shape[0] // 2, HALVES * one.shape[1]), BF16)
    return pl.pallas_call(
        finish_body,
        in_specs=[vmem] * (2 + len(terms)),
        out_specs=[vmem, vmem],
        out_shape=[out, out],
        compiler_params=pltpu.CompilerParams(vmem_limit_bytes=VMEM_LIMIT),
        cost_estimate=pl.CostEstimate(flops=2**19, bytes_accessed=2**21, transcendentals=0),
        name="finish",
    )(one, two, *terms)


def table_part(section_count, gathered):
    count = gathered.shape[0]
    lanes = lane_iota((count, LANES))
    column = jnp.where(lanes < NB, lanes, lanes - NB).astype(F32)
    section = jnp.right_shift(lanes, 4)
    high = gathered.astype(BF16)
    low = (gathered - high.astype(F32)).astype(BF16)
    row_hot = (lane_iota((count, NB)).astype(F32) == gathered[:, BUCKET_LANE : BUCKET_LANE + 1]).astype(BF16)
    spread = jnp.bitwise_and(row_iota((LANES, H * NB)), H - 1) == jnp.right_shift(
        lane_iota((LANES, H * NB)), 6
    )
    spread = jnp.where(spread, 1.0, 0.0).astype(BF16)
    pieces = []
    for s in range(section_count):
        for part in (high, low):
            pieces.append(jnp.where(section == s, part, jnp.zeros_like(part)))
    wide = contract(jnp.concatenate(pieces, axis=0), spread, 1, 0)
    masked = []
    for s in range(section_count):
        hot = column == gathered[:, BUCKET_LANE + s : BUCKET_LANE + s + 1]
        hot = jnp.concatenate([hot.astype(F32)] * (H * NB // LANES), axis=1)
        for part in range(2):
            start = (2 * s + part) * count
            masked.append((wide[start : start + count] * hot).astype(BF16))
    rows = jnp.concatenate([row_hot] * (2 * section_count), axis=0)
    return rows, jnp.concatenate(masked, axis=0)


def table_body(section_count, gathered_ref, table_ref, scratch, total, staged, sems):
    count = gathered_ref.shape[0]

    def copy_row(row, carry):
        scratch[pl.ds(row, 1), :] = gathered_ref[row]
        return carry

    lax.fori_loop(0, count, copy_row, 0, unroll=8)
    if count <= TABLE_ROWS:
        rows, spread = table_part(section_count, scratch[...])

        def columns(window):
            return contract(rows, spread[:, window], 0, 0)

    else:
        total[...] = jnp.zeros_like(total)

        def add_part(step, carry):
            start = pl.multiple_of(step * TABLE_ROWS, TABLE_ROWS)
            rows, spread = table_part(section_count, scratch[pl.ds(start, TABLE_ROWS), :])
            total[...] += contract(rows, spread, 0, 0)
            return carry

        lax.fori_loop(0, count // TABLE_ROWS, add_part, 0)

        def columns(window):
            return total[:, window]

    copies = []
    for group in range(H // TABLE_HEADS):
        part = columns(slice(group * TABLE_HEADS * NB, (group + 1) * TABLE_HEADS * NB))
        heads = pl.ds(group * TABLE_HEADS, TABLE_HEADS)
        for head in range(TABLE_HEADS):
            staged[group * TABLE_HEADS + head] = part[:, head * NB : (head + 1) * NB]
        copies.append(
            pltpu.make_async_copy(staged.at[heads], table_ref.at[heads], sems.at[group])
        )
        copies[-1].start()
    for copy in copies:
        copy.wait()


def table_of(gathered, section_count):
    vmem = pl.BlockSpec(memory_space=pltpu.VMEM)
    return pl.pallas_call(
        functools.partial(table_body, section_count),
        in_specs=[vmem],
        out_specs=pl.BlockSpec(memory_space=pltpu.HBM),
        out_shape=jax.ShapeDtypeStruct((H, NB, NB), F32),
        scratch_shapes=[
            pltpu.VMEM((gathered.shape[0], LANES), F32),
            pltpu.VMEM((NB, H * NB), F32),
            pltpu.VMEM((H, NB, NB), F32),
            pltpu.SemaphoreType.DMA((H // TABLE_HEADS,)),
        ],
        compiler_params=pltpu.CompilerParams(vmem_limit_bytes=VMEM_LIMIT),
        name="table",
    )(gathered)


def in_hbm(array):
    return pltpu.with_memory_space_constraint(array, pltpu.HBM)


def pack_body(*refs):
    bucket_hbm, seg_hbm, key_hbm, value_hbm, first_ref, seg_ref, bucket_ref, sems = refs
    pairs = (first_ref.shape[0] - INFO) // (2 * BLK)
    small = [(bucket_hbm, bucket_ref), (seg_hbm, seg_ref)]
    copies = [
        pltpu.make_async_copy(source, target, sems.at[i]) for i, (source, target) in enumerate(small)
    ]
    for pair in range(pairs):
        for row, source in ((0, key_hbm), (BLK, value_hbm)):
            copies.append(
                pltpu.make_async_copy(
                    source.at[:, pl.ds(pair * PAIR_LANES, PAIR_LANES)],
                    first_ref.at[pl.ds(pair * 2 * BLK + row, BLK), :],
                    sems.at[len(copies)],
                )
            )
    for copy in copies:
        copy.start()
    for copy in copies[: len(small)]:
        copy.wait()
    top = row_iota((INFO, LANES)) == 0
    bucket = jnp.broadcast_to(bucket_ref[...], (INFO, LANES))
    info = jnp.where(top, seg_ref[...], bucket).astype(F32).astype(BF16)
    first_ref[pairs * 2 * BLK : pairs * 2 * BLK + INFO, :] = info
    for copy in copies[len(small) :]:
        copy.wait()


def pack(bucket, seg, keys, values):
    pairs = keys.shape[1] // HALVES // PAIR_LANES
    vmem = pl.BlockSpec(memory_space=pltpu.VMEM)
    hbm = pl.BlockSpec(memory_space=pltpu.HBM)
    return pl.pallas_call(
        pack_body,
        in_specs=[pl.BlockSpec(memory_space=pl.ANY), hbm, hbm, hbm],
        out_specs=[vmem] * 2,
        out_shape=[
            jax.ShapeDtypeStruct((pairs * 2 * BLK + INFO, PAIR_LANES), BF16),
            jax.ShapeDtypeStruct(seg.shape, jnp.int32),
        ],
        scratch_shapes=[
            pltpu.VMEM(bucket.shape, jnp.int32),
            pltpu.SemaphoreType.DMA((2 + 2 * pairs,)),
        ],
        compiler_params=pltpu.CompilerParams(vmem_limit_bytes=VMEM_LIMIT),
        name="pack",
    )(bucket, *[in_hbm(a) for a in (seg, keys, values)])


def load_body(first_ref, *refs):
    mask_hbm, *sources = refs[:6]
    param_ref, *targets = refs[6:12]
    mask_ref, sems = refs[12:]
    whole_ref, second_ref = targets[:2]
    pairs = second_ref.shape[0] // (2 * BLK)
    copies = []

    def add(source, target):
        copies.append(pltpu.make_async_copy(source, target, sems.at[len(copies)]))
        copies[-1].start()

    add(mask_hbm, mask_ref)
    for row, source in ((0, sources[0]), (BLK, sources[1])):
        for pair in range(pairs):
            window = pl.ds((pairs + pair) * PAIR_LANES, PAIR_LANES)
            add(source.at[:, window], second_ref.at[pl.ds(pair * 2 * BLK + row, BLK), :])
        add(source, whole_ref.at[pl.ds(row, BLK), :])
    for source, target in zip(sources[2:], targets[2:]):
        add(source, target)
    copies[0].wait()
    lines = row_iota((2 * INFO, LANES))
    bucket = first_ref[pairs * 2 * BLK : pairs * 2 * BLK + INFO, :].astype(F32)[1:2]
    params = jnp.where(lines == INFO, bucket, 0.0)
    for s in range(1, mask_ref.shape[1]):
        shut = jnp.where(mask_ref[:, s : s + 1] != 0, 0.0, MASKED)
        params = jnp.where(lines == s, shut, params)
    param_ref[...] = params
    for copy in copies[1:]:
        copy.wait()


def load(first, mask, keys, values, *arrays):
    row_count, feature_count = keys.shape
    pairs = feature_count // HALVES // PAIR_LANES
    vmem = pl.BlockSpec(memory_space=pltpu.VMEM)
    out_shape = [
        jax.ShapeDtypeStruct((2 * INFO, LANES), F32),
        jax.ShapeDtypeStruct((2 * row_count, feature_count), BF16),
        jax.ShapeDtypeStruct((pairs * 2 * BLK, PAIR_LANES), BF16),
        *[jax.ShapeDtypeStruct(a.shape, a.dtype) for a in arrays],
    ]
    return pl.pallas_call(
        load_body,
        in_specs=[vmem] + [pl.BlockSpec(memory_space=pltpu.HBM)] * 6,
        out_specs=[vmem] * 6,
        out_shape=out_shape,
        scratch_shapes=[
            pltpu.VMEM(mask.shape, jnp.int32),
            pltpu.SemaphoreType.DMA((3 + 2 * pairs + len(arrays),)),
        ],
        compiler_params=pltpu.CompilerParams(vmem_limit_bytes=VMEM_LIMIT),
        name="load",
    )(first, *[in_hbm(a) for a in (mask, keys, values, *arrays)])


def after(value, *earlier):
    return lax.optimization_barrier((value, *earlier))[0]


def double(block, axis, mask):
    return jnp.concatenate([block, from_partner(block, axis, mask)], axis=0)


def local(queries, keys, values, d_out, segment_ids, block_bucket, block_mask, bias_table):
    level_count = lax.axis_size("seq").bit_length() - 1
    far_levels = list(range(level_count))
    last = far_levels[-2:]

    def send(value, level):
        return from_partner(value, "seq", 1 << level)

    first, seg = pack(block_bucket, segment_ids, keys[0], values[0])
    params, whole, second, query_rows, grad_rows, table_rows = load(
        first,
        block_mask.reshape(1, -1),
        keys[0],
        values[0],
        queries[0],
        d_out[0],
        bias_table.reshape(H * NB, NB),
    )
    scalars = (seg, params)
    rows = [query_rows, grad_rows, whole]
    far = [{}, {}]
    for level in reversed(far_levels):
        far[0][level] = send(first, level)
    for level in far_levels:
        gate = (far[0][0], query_rows) if level else (far[0][last[-1]], query_rows)
        far[1][level] = send(after(second, *gate), level)
    near_list = []
    near_count = len(near_list)

    device_count = lax.axis_size("dp") * lax.axis_size("seq")
    one = attention_half(
        0, device_count, scalars, table_rows, rows, near_list, [far[0][level] for level in far_levels], None
    )
    middle = [level for level in range(level_count) if level not in last]
    terms = one[3 : 3 + level_count]
    back_one = {level: send(terms[level], level) for level in [*last, *middle[1:]]}
    late = [back_one[level] for level in last]
    two = attention_half(
        1, device_count, scalars, table_rows, rows, near_list, [far[1][level] for level in far_levels], one
    )
    terms = two[3 : 3 + level_count]
    back_two = {level: send(terms[level], level) for level in last}
    block = two[3 + level_count]
    gathered = lax.all_to_all(block, ("dp", "seq"), 0, 0, tiled=True)
    for level in middle:
        back_two[level] = send(after(terms[level], *late, *[back_one[m] for m in middle[1:]]), level)
    back_one[0] = send(after(one[3], *late), 0)
    sum_one = gather_terms(one[2], list(back_one.values()))
    sum_two = gather_terms(two[2], [back_two[level] for level in last])
    d_keys, d_values = finish(sum_one, sum_two, [back_two[level] for level in middle])
    table_total = table_of(after(gathered, d_keys), level_count + 1)
    return (two[0][None], two[1][None], d_keys[None], d_values[None], table_total)


def solution(mesh):
    rows = P("dp", "seq", None)
    in_specs = (
        rows,
        rows,
        rows,
        rows,
        P("dp", "seq"),
        P("dp", "seq"),
        P("dp", "seq", None, None),
        P(),
    )
    return jax.shard_map(
        local, mesh=mesh, in_specs=in_specs, out_specs=(rows,) * 4 + (P(),), check_vma=False
    )
```

```python
import functools

import jax
import jax.numpy as jnp
from jax import lax
from jax.experimental import pallas as pl
from jax.experimental.pallas import tpu as pltpu
from jax.sharding import PartitionSpec as P

H = 16
DH = 64
NB = 64
BLK = 128
HALVES = 2
INFO = 8
LANES = 128
PAIR_LANES = 2 * DH
BUCKET_LANE = 112
MASKED = -1e30
TABLE_ROWS = 32
TABLE_HEADS = 4
UNROLL = 4
VMEM_LIMIT = 10 * 2**20
FLOPS = 2 * 10**10

F32 = jnp.float32
BF16 = jnp.bfloat16


def contract(a, b, dim_a, dim_b):
    return lax.dot_general(a, b, (((dim_a,), (dim_b,)), ((), ())), preferred_element_type=F32)


def from_partner(value, axis, mask):
    pairs = [(source, source ^ mask) for source in range(lax.axis_size(axis))]
    return lax.ppermute(value, axis, pairs)


def lane_iota(shape):
    return lax.broadcasted_iota(jnp.int32, shape, len(shape) - 1)


def row_iota(shape):
    return lax.broadcasted_iota(jnp.int32, shape, len(shape) - 2)


def split_pair(pair, low):
    zero = jnp.zeros_like(pair)
    return jnp.concatenate([jnp.where(low, pair, zero), jnp.where(low, zero, pair)], axis=0)


def attention_body(near_count, far_count, half, *refs):
    section_count = 1 + near_count + far_count
    first = half == 0
    refs = list(refs)

    def take(count):
        taken, refs[:] = refs[:count], refs[count:]
        return taken

    seg_ref, param_ref, table_ref, q_ref, do_ref, own_pack_ref = take(6)
    near_refs = take(near_count)
    far_refs = take(far_count)
    if not first:
        masks, biases, pay_in_ref = take(3)
        earlier = take(2)
    out_ref, dq_ref = take(2)
    own_ref, *term_refs, pay_ref = take(1 + section_count)
    if first:
        masks, biases = take(2)
    half_features = own_ref.shape[1]
    half_heads = half_features // DH
    info_row = half_features // PAIR_LANES * 2 * BLK

    if first:
        own_bucket = param_ref[INFO : INFO + 1, :]
        seg_rows = seg_ref[...].astype(F32)
        in_row = row_iota((H, NB, LANES)).astype(F32) == own_bucket
        pay = jnp.zeros((1, LANES), F32)
        for s in range(section_count):
            if s == 0:
                seg_cols = seg_rows
                bucket = own_bucket
            else:
                info = far_refs[s - 1][info_row : info_row + INFO, :].astype(F32)
                seg_cols = info[0:1]
                bucket = info[1:2]
            cols = jnp.broadcast_to(seg_cols, (BLK, BLK)).T
            masks[s * BLK : (s + 1) * BLK, :] = jnp.where(
                cols == seg_rows, jnp.broadcast_to(param_ref[s : s + 1, :], (BLK, BLK)), MASKED
            )
            hot = (row_iota((NB, LANES)).astype(F32) == bucket).astype(BF16)
            picked = contract(table_ref[...], hot, 1, 0).reshape(H, NB, LANES)
            biases[s] = jnp.sum(jnp.where(in_row, picked, 0.0), axis=1)
            pay = jnp.where(lane_iota(pay.shape) == BUCKET_LANE + s, bucket, pay)
        pay_ref[0] = pay
    else:
        pay_ref[0] = pay_in_ref[0]
        for source, target in zip(earlier, [out_ref, dq_ref]):
            target[:, 0 : half * half_features] = source[...]

    low = lane_iota((BLK, PAIR_LANES)) < DH
    lanes = lane_iota((1, LANES))

    def one_pair(pair, carry):
        here = pl.ds(pl.multiple_of(pair * PAIR_LANES, PAIR_LANES), PAIR_LANES)
        there = pl.ds(
            pl.multiple_of(half * half_features + pair * PAIR_LANES, PAIR_LANES), PAIR_LANES
        )
        mine = here if first else there
        key_block = pl.ds(pl.multiple_of(pair * 2 * BLK, BLK), BLK)
        value_block = pl.ds(pl.multiple_of(pair * 2 * BLK + BLK, BLK), BLK)
        head = half * half_heads + 2 * pair
        q_stack = split_pair(q_ref[:, there] * jnp.asarray(0.125, BF16), low)
        grad_stack = split_pair(do_ref[:, there], low)
        key_rows = jnp.concatenate(
            [own_pack_ref[0:BLK, there]]
            + [r[key_block, :] for r in far_refs],
            axis=0,
        )
        value_rows = jnp.concatenate(
            [own_pack_ref[BLK : 2 * BLK, there]]
            + [r[value_block, :] for r in far_refs],
            axis=0,
        )
        raw = contract(key_rows, q_stack, 1, 1)
        dprob = contract(value_rows, grad_stack, 1, 1)
        scores = []
        shifts = []
        top = None
        for s in range(section_count):
            block = slice(s * BLK, (s + 1) * BLK)
            mask = masks[block, :]
            score = raw[block] + jnp.concatenate([mask, mask], axis=1)
            bias = jnp.concatenate(
                [biases[s, pl.ds(head, 1), :], biases[s, pl.ds(head + 1, 1), :]], axis=1
            )
            best = jnp.max(score, axis=0, keepdims=True) + bias
            top = best if top is None else jnp.maximum(top, best)
            scores.append(score)
            shifts.append(bias)
        weights = [jnp.exp(scores[s] - (top - shifts[s])) for s in range(section_count)]
        total = sum(jnp.sum(weight, axis=0, keepdims=True) for weight in weights)
        inverse = 1.0 / total
        probs = [weight * inverse for weight in weights]
        probs_low = jnp.concatenate([prob.astype(BF16) for prob in probs], axis=0)
        out_stack = contract(probs_low, value_rows, 0, 0)
        pulls = [probs[s] * dprob[s * BLK : (s + 1) * BLK] for s in range(section_count)]
        delta = sum(jnp.sum(pull, axis=0, keepdims=True) for pull in pulls)
        dscores = [pulls[s] - probs[s] * delta for s in range(section_count)]
        dscore_low = jnp.concatenate([dscore.astype(BF16) for dscore in dscores], axis=0)
        value_terms = contract(probs_low, grad_stack, 1, 0)
        key_terms = contract(dscore_low, q_stack, 1, 0)
        dq_stack = contract(dscore_low, key_rows, 0, 0)
        out_ref[:, mine] = jnp.where(low, out_stack[:BLK], out_stack[BLK:]).astype(BF16)
        dq_ref[:, mine] = (jnp.where(low, dq_stack[:BLK], dq_stack[BLK:]) * 0.125).astype(BF16)
        pay = pay_ref[0]
        for s in range(section_count):
            sums = jnp.sum(dscores[s], axis=0, keepdims=True)
            even = jnp.sum(sums[:, :BLK], axis=1, keepdims=True)
            odd = jnp.sum(sums[:, BLK:], axis=1, keepdims=True)
            pay = jnp.where(lanes == s * H + head, even, pay)
            pay = jnp.where(lanes == s * H + head + 1, odd, pay)
            key_term = key_terms[s * BLK : (s + 1) * BLK]
            value_term = value_terms[s * BLK : (s + 1) * BLK]
            if s == 0:
                own_ref[0:BLK, here] = key_term
                own_ref[BLK : 2 * BLK, here] = value_term
            else:
                term_refs[s - 1][0:BLK, here] = key_term.astype(BF16)
                term_refs[s - 1][BLK : 2 * BLK, here] = value_term.astype(BF16)
        pay_ref[...] = jnp.broadcast_to(pay[:, None, :], pay_ref.shape)
        return carry

    lax.fori_loop(0, half_features // PAIR_LANES, one_pair, 0, unroll=UNROLL)


def attention_half(half, copies, scalars, table_rows, rows, near, far, previous):
    near_count, far_count = len(near), len(far)
    section_count = 1 + near_count + far_count
    row_count, feature_count = rows[0].shape
    half_features = feature_count // HALVES
    half_heads = half_features // DH
    vmem = pl.BlockSpec(memory_space=pltpu.VMEM)
    operands = [*scalars, table_rows, *rows, *near, *far]
    in_specs = [vmem] * len(operands)
    covered = (half + 1) * half_features
    packed = jax.ShapeDtypeStruct((2 * row_count, half_features), BF16)
    out_shape = [
        *[jax.ShapeDtypeStruct((row_count, covered), BF16)] * 2,
        jax.ShapeDtypeStruct((2 * row_count, half_features), F32),
        *[packed] * (section_count - 1),
        jax.ShapeDtypeStruct((1 if previous is None else copies, 1, LANES), F32),
    ]
    if previous is None:
        out_shape += [
            jax.ShapeDtypeStruct((section_count * BLK, BLK), F32),
            jax.ShapeDtypeStruct((section_count, H, LANES), F32),
        ]
    else:
        operands += [*previous[-2:], previous[-3], *previous[:2]]
        in_specs += [vmem] * 5
    return pl.pallas_call(
        functools.partial(attention_body, near_count, far_count, half),
        in_specs=in_specs,
        out_specs=[vmem] * len(out_shape),
        out_shape=out_shape,
        compiler_params=pltpu.CompilerParams(vmem_limit_bytes=VMEM_LIMIT),
        cost_estimate=pl.CostEstimate(
            flops=FLOPS, bytes_accessed=4 * 2**20, transcendentals=section_count * half_heads * BLK * BLK
        ),
        name="attention",
    )(*operands)


def gather_body(*refs):
    total = refs[0][...]
    for ref in refs[1:-1]:
        total = total + ref[...].astype(F32)
    refs[-1][...] = total


def gather_terms(own, terms):
    vmem = pl.BlockSpec(memory_space=pltpu.VMEM)
    return pl.pallas_call(
        gather_body,
        in_specs=[vmem] * (1 + len(terms)),
        out_specs=vmem,
        out_shape=jax.ShapeDtypeStruct(own.shape, F32),
        compiler_params=pltpu.CompilerParams(vmem_limit_bytes=VMEM_LIMIT),
        cost_estimate=pl.CostEstimate(flops=2**19, bytes_accessed=2**21, transcendentals=0),
        name="gather",
    )(own, *terms)


def finish_body(*refs):
    one_ref, two_ref, *term_refs = refs[:-2]
    half_features = one_ref.shape[1]
    for out_ref, block in zip(refs[-2:], (slice(0, BLK), slice(BLK, 2 * BLK))):
        out_ref[:, :half_features] = one_ref[block, :].astype(BF16)
        total = two_ref[block, :]
        for ref in term_refs:
            total = total + ref[block, :].astype(F32)
        out_ref[:, half_features:] = total.astype(BF16)


def finish(one, two, terms):
    vmem = pl.BlockSpec(memory_space=pltpu.VMEM)
    out = jax.ShapeDtypeStruct((one.shape[0] // 2, HALVES * one.shape[1]), BF16)
    return pl.pallas_call(
        finish_body,
        in_specs=[vmem] * (2 + len(terms)),
        out_specs=[vmem, vmem],
        out_shape=[out, out],
        compiler_params=pltpu.CompilerParams(vmem_limit_bytes=VMEM_LIMIT),
        cost_estimate=pl.CostEstimate(flops=2**19, bytes_accessed=2**21, transcendentals=0),
        name="finish",
    )(one, two, *terms)


def table_part(section_count, gathered):
    count = gathered.shape[0]
    lanes = lane_iota((count, LANES))
    column = jnp.where(lanes < NB, lanes, lanes - NB).astype(F32)
    section = jnp.right_shift(lanes, 4)
    high = gathered.astype(BF16)
    low = (gathered - high.astype(F32)).astype(BF16)
    row_hot = (lane_iota((count, NB)).astype(F32) == gathered[:, BUCKET_LANE : BUCKET_LANE + 1]).astype(BF16)
    spread = jnp.bitwise_and(row_iota((LANES, H * NB)), H - 1) == jnp.right_shift(
        lane_iota((LANES, H * NB)), 6
    )
    spread = jnp.where(spread, 1.0, 0.0).astype(BF16)
    pieces = []
    for s in range(section_count):
        for part in (high, low):
            pieces.append(jnp.where(section == s, part, jnp.zeros_like(part)))
    wide = contract(jnp.concatenate(pieces, axis=0), spread, 1, 0)
    masked = []
    for s in range(section_count):
        hot = column == gathered[:, BUCKET_LANE + s : BUCKET_LANE + s + 1]
        hot = jnp.concatenate([hot.astype(F32)] * (H * NB // LANES), axis=1)
        for part in range(2):
            start = (2 * s + part) * count
            masked.append((wide[start : start + count] * hot).astype(BF16))
    rows = jnp.concatenate([row_hot] * (2 * section_count), axis=0)
    return rows, jnp.concatenate(masked, axis=0)


def table_body(section_count, gathered_ref, table_ref, scratch, total, staged, sems):
    count = gathered_ref.shape[0]

    def copy_row(row, carry):
        scratch[pl.ds(row, 1), :] = gathered_ref[row]
        return carry

    lax.fori_loop(0, count, copy_row, 0, unroll=8)
    if count <= TABLE_ROWS:
        rows, spread = table_part(section_count, scratch[...])

        def columns(window):
            return contract(rows, spread[:, window], 0, 0)

    else:
        total[...] = jnp.zeros_like(total)

        def add_part(step, carry):
            start = pl.multiple_of(step * TABLE_ROWS, TABLE_ROWS)
            rows, spread = table_part(section_count, scratch[pl.ds(start, TABLE_ROWS), :])
            total[...] += contract(rows, spread, 0, 0)
            return carry

        lax.fori_loop(0, count // TABLE_ROWS, add_part, 0)

        def columns(window):
            return total[:, window]

    copies = []
    for group in range(H // TABLE_HEADS):
        part = columns(slice(group * TABLE_HEADS * NB, (group + 1) * TABLE_HEADS * NB))
        heads = pl.ds(group * TABLE_HEADS, TABLE_HEADS)
        for head in range(TABLE_HEADS):
            staged[group * TABLE_HEADS + head] = part[:, head * NB : (head + 1) * NB]
        copies.append(
            pltpu.make_async_copy(staged.at[heads], table_ref.at[heads], sems.at[group])
        )
        copies[-1].start()
    for copy in copies:
        copy.wait()


def table_of(gathered, section_count):
    vmem = pl.BlockSpec(memory_space=pltpu.VMEM)
    return pl.pallas_call(
        functools.partial(table_body, section_count),
        in_specs=[vmem],
        out_specs=pl.BlockSpec(memory_space=pltpu.HBM),
        out_shape=jax.ShapeDtypeStruct((H, NB, NB), F32),
        scratch_shapes=[
            pltpu.VMEM((gathered.shape[0], LANES), F32),
            pltpu.VMEM((NB, H * NB), F32),
            pltpu.VMEM((H, NB, NB), F32),
            pltpu.SemaphoreType.DMA((H // TABLE_HEADS,)),
        ],
        compiler_params=pltpu.CompilerParams(vmem_limit_bytes=VMEM_LIMIT),
        name="table",
    )(gathered)


def in_hbm(array):
    return pltpu.with_memory_space_constraint(array, pltpu.HBM)


def pack_body(*refs):
    bucket_hbm, seg_hbm, key_hbm, value_hbm, first_ref, seg_ref, bucket_ref, sems = refs
    pairs = (first_ref.shape[0] - INFO) // (2 * BLK)
    small = [(bucket_hbm, bucket_ref), (seg_hbm, seg_ref)]
    copies = [
        pltpu.make_async_copy(source, target, sems.at[i]) for i, (source, target) in enumerate(small)
    ]
    for pair in range(pairs):
        for row, source in ((0, key_hbm), (BLK, value_hbm)):
            copies.append(
                pltpu.make_async_copy(
                    source.at[:, pl.ds(pair * PAIR_LANES, PAIR_LANES)],
                    first_ref.at[pl.ds(pair * 2 * BLK + row, BLK), :],
                    sems.at[len(copies)],
                )
            )
    for copy in copies:
        copy.start()
    for copy in copies[: len(small)]:
        copy.wait()
    top = row_iota((INFO, LANES)) == 0
    bucket = jnp.broadcast_to(bucket_ref[...], (INFO, LANES))
    info = jnp.where(top, seg_ref[...], bucket).astype(F32).astype(BF16)
    first_ref[pairs * 2 * BLK : pairs * 2 * BLK + INFO, :] = info
    for copy in copies[len(small) :]:
        copy.wait()


def pack(bucket, seg, keys, values):
    pairs = keys.shape[1] // HALVES // PAIR_LANES
    vmem = pl.BlockSpec(memory_space=pltpu.VMEM)
    hbm = pl.BlockSpec(memory_space=pltpu.HBM)
    return pl.pallas_call(
        pack_body,
        in_specs=[pl.BlockSpec(memory_space=pl.ANY), hbm, hbm, hbm],
        out_specs=[vmem] * 2,
        out_shape=[
            jax.ShapeDtypeStruct((pairs * 2 * BLK + INFO, PAIR_LANES), BF16),
            jax.ShapeDtypeStruct(seg.shape, jnp.int32),
        ],
        scratch_shapes=[
            pltpu.VMEM(bucket.shape, jnp.int32),
            pltpu.SemaphoreType.DMA((2 + 2 * pairs,)),
        ],
        compiler_params=pltpu.CompilerParams(vmem_limit_bytes=VMEM_LIMIT),
        name="pack",
    )(bucket, *[in_hbm(a) for a in (seg, keys, values)])


def load_body(first_ref, *refs):
    mask_hbm, *sources = refs[:6]
    param_ref, *targets = refs[6:12]
    mask_ref, sems = refs[12:]
    whole_ref, second_ref = targets[:2]
    pairs = second_ref.shape[0] // (2 * BLK)
    copies = []

    def add(source, target):
        copies.append(pltpu.make_async_copy(source, target, sems.at[len(copies)]))
        copies[-1].start()

    add(mask_hbm, mask_ref)
    for row, source in ((0, sources[0]), (BLK, sources[1])):
        for pair in range(pairs):
            window = pl.ds((pairs + pair) * PAIR_LANES, PAIR_LANES)
            add(source.at[:, window], second_ref.at[pl.ds(pair * 2 * BLK + row, BLK), :])
        add(source, whole_ref.at[pl.ds(row, BLK), :])
    for source, target in zip(sources[2:], targets[2:]):
        add(source, target)
    copies[0].wait()
    lines = row_iota((2 * INFO, LANES))
    bucket = first_ref[pairs * 2 * BLK : pairs * 2 * BLK + INFO, :].astype(F32)[1:2]
    params = jnp.where(lines == INFO, bucket, 0.0)
    for s in range(1, mask_ref.shape[1]):
        shut = jnp.where(mask_ref[:, s : s + 1] != 0, 0.0, MASKED)
        params = jnp.where(lines == s, shut, params)
    param_ref[...] = params
    for copy in copies[1:]:
        copy.wait()


def load(first, mask, keys, values, *arrays):
    row_count, feature_count = keys.shape
    pairs = feature_count // HALVES // PAIR_LANES
    vmem = pl.BlockSpec(memory_space=pltpu.VMEM)
    out_shape = [
        jax.ShapeDtypeStruct((2 * INFO, LANES), F32),
        jax.ShapeDtypeStruct((2 * row_count, feature_count), BF16),
        jax.ShapeDtypeStruct((pairs * 2 * BLK, PAIR_LANES), BF16),
        *[jax.ShapeDtypeStruct(a.shape, a.dtype) for a in arrays],
    ]
    return pl.pallas_call(
        load_body,
        in_specs=[vmem] + [pl.BlockSpec(memory_space=pltpu.HBM)] * 6,
        out_specs=[vmem] * 6,
        out_shape=out_shape,
        scratch_shapes=[
            pltpu.VMEM(mask.shape, jnp.int32),
            pltpu.SemaphoreType.DMA((3 + 2 * pairs + len(arrays),)),
        ],
        compiler_params=pltpu.CompilerParams(vmem_limit_bytes=VMEM_LIMIT),
        name="load",
    )(first, *[in_hbm(a) for a in (mask, keys, values, *arrays)])


def after(value, *earlier):
    return lax.optimization_barrier((value, *earlier))[0]


def double(block, axis, mask):
    return jnp.concatenate([block, from_partner(block, axis, mask)], axis=0)


def local(queries, keys, values, d_out, segment_ids, block_bucket, block_mask, bias_table):
    level_count = lax.axis_size("seq").bit_length() - 1
    far_levels = list(range(level_count))
    last = far_levels[-2:]

    def send(value, level):
        return from_partner(value, "seq", 1 << level)

    first, seg = pack(block_bucket, segment_ids, keys[0], values[0])
    params, whole, second, query_rows, grad_rows, table_rows = load(
        first,
        block_mask.reshape(1, -1),
        keys[0],
        values[0],
        queries[0],
        d_out[0],
        bias_table.reshape(H * NB, NB),
    )
    scalars = (seg, params)
    rows = [query_rows, grad_rows, whole]
    far = [{}, {}]
    for level in reversed(far_levels):
        far[0][level] = send(first, level)
    for level in far_levels:
        gate = (far[0][0], query_rows) if level else (far[0][last[-1]], query_rows)
        far[1][level] = send(after(second, *gate), level)
    near_list = []
    near_count = len(near_list)

    device_count = lax.axis_size("dp") * lax.axis_size("seq")
    one = attention_half(
        0, device_count, scalars, table_rows, rows, near_list, [far[0][level] for level in far_levels], None
    )
    middle = [level for level in range(level_count) if level not in last]
    terms = one[3 : 3 + level_count]
    back_one = {level: send(terms[level], level) for level in [*last, *middle[1:]]}
    late = [back_one[level] for level in last]
    two = attention_half(
        1, device_count, scalars, table_rows, rows, near_list, [far[1][level] for level in far_levels], one
    )
    terms = two[3 : 3 + level_count]
    back_two = {level: send(terms[level], level) for level in last}
    block = two[3 + level_count]
    gathered = lax.all_to_all(block, ("dp", "seq"), 0, 0, tiled=True)
    for level in middle:
        back_two[level] = send(after(terms[level], *late, *[back_one[m] for m in middle[1:]]), level)
    back_one[0] = send(after(one[3], *late), 0)
    sum_one = gather_terms(one[2], list(back_one.values()))
    sum_two = gather_terms(two[2], [back_two[level] for level in last])
    d_keys, d_values = finish(sum_one, sum_two, [back_two[level] for level in middle])
    table_total = table_of(after(gathered, d_keys), level_count + 1)
    return (two[0][None], two[1][None], d_keys[None], d_values[None], table_total)


def solution(mesh):
    rows = P("dp", "seq", None)
    in_specs = (
        rows,
        rows,
        rows,
        rows,
        P("dp", "seq"),
        P("dp", "seq"),
        P("dp", "seq", None, None),
        P(),
    )
    return jax.shard_map(
        local, mesh=mesh, in_specs=in_specs, out_specs=(rows,) * 4 + (P(),), check_vma=False
    )
```
